32 devices in a mesh: col: 8 (over z, y), row: 4 (over x, core).
Axes of the slice: x: 2, y: 2, z: 4, core: 2. Of those that a mesh axis runs over, the one named last changes fastest.
Arguments:
- right_side: float32 [32, 256], P(('row', 'col')), may hold values from -6 to 6
- precond: float32 [32, 256], P(('row', 'col')), may hold values from 0.3 to 3
- scaling: float32 [64, 256], P('col'), may hold values from 0.1 to 10
- blocks: float32 [8, 4, 16, 256, 256], P('col', 'row'), may hold values from -0.09375 to 0.09375
- block_count: int32 [8, 4], P('col', 'row'), may hold values from 5 to 16, as said below
- block_rows: int32 [8, 4, 16], P('col', 'row'), may hold values from 0 to 7
- block_cols: int32 [8, 4, 16], P('col', 'row'), may hold values from 0 to 7
Outputs:
- solution_field: float32 [32, 256], P(('row', 'col'))
- residual: float32 [32, 256], P(('row', 'col'))
The draws below stay inside these ranges and needn't reach their ends.
Inputs may be any that keep to these rules, and one draw needn't show every extreme that they name: `block_count`: each device has between 5 and 16 live slots; device (0, 0) has 16.
All inputs are finite; a program needn't handle non-finite values.
Results may differ from the reference program's by a relative error of at most 0.0003.
Values sent between devices are 32-bit elements; how exact they have to be, the bound alone decides.
No kernel may reach another device: no remote copies, remote signals or barrier semaphores. Data moves between devices by JAX's collectives and lax.ppermute only.
A program may use at most 64 MiB of HBM per device.

```python
import math
import jax
import jax.numpy as jnp
from jax import lax

BS = 256
CB_DEV = 8
NB = 16
ITERS = 2
COL_DEVS = 8
ROW_DEVS = 4
GROUP_ROWS = 8
RBLOCKS = 32
CBLOCKS = 64


def draw_block_count(key, part):
    subkey = jax.random.fold_in(key, 11)
    counts = jax.random.randint(subkey, (COL_DEVS, ROW_DEVS), NB // 3, NB + 1)
    counts = counts.at[0, 0].set(NB).at[0, 1].set(NB // 3)
    return counts.astype(jnp.int32)


def draw_block_rows(key, part):
    subkey = jax.random.fold_in(key, 12)
    rows = jax.random.randint(subkey, (COL_DEVS, ROW_DEVS, NB), 0, GROUP_ROWS)
    rows = rows.at[0, 0, 0].set(0).at[0, 0, 1].set(GROUP_ROWS - 1)
    return rows.astype(jnp.int32)


def draw_block_cols(key, part):
    subkey = jax.random.fold_in(key, 13)
    cols = jax.random.randint(subkey, (COL_DEVS, ROW_DEVS, NB), 0, CB_DEV)
    cols = cols.at[0, 0, 0].set(0).at[0, 0, 1].set(CB_DEV - 1)
    return cols.astype(jnp.int32)


def steps_of(stream_key, extent, cuts, smallest, top_value):
    def one(dim, blocks):
        steps = jax.random.uniform(jax.random.fold_in(jax.random.fold_in(stream_key, 6), dim), (blocks,), jnp.float32, smallest / len(cuts), top_value / len(cuts))
        return jnp.repeat(jnp.exp(steps), extent[dim] // blocks).reshape((-1,) + (1,) * (len(extent) - dim - 1))

    loudness = one(*cuts[0])
    for cut in cuts[1:]:
        loudness = loudness * one(*cut)
    return loudness


def normal_values(key, extent, width, limit, pieces=(), kind=jnp.bfloat16):
    gain = steps_of(key, extent, pieces, -0.22, 0.18) if pieces else 1.0
    values = jax.random.normal(key, extent, jnp.float32) * width * gain
    return jnp.minimum(jnp.maximum(values, -limit), limit).astype(kind)


def setup_inputs(seed: int = 0) -> dict:
    seeds = jax.random.split(jax.random.key(seed), 8)
    return {
        "right_side": normal_values(seeds[0], (RBLOCKS, BS), 1.0, 6.0, ((0, 32),), jnp.float32),
        "precond": jnp.clip(jnp.exp(math.log(3.0) - 2.3025851 * jax.random.uniform(seeds[1], (RBLOCKS, BS), jnp.float32) ** steps_of(seeds[1], (RBLOCKS, BS), ((0, 32),), -0.2, 0.2)), 0.3, 3.0),
        "scaling": jnp.clip(jnp.exp(math.log(10.0) - 4.6051702 * jax.random.uniform(seeds[2], (CBLOCKS, BS), jnp.float32) ** steps_of(seeds[2], (CBLOCKS, BS), ((0, 8),), -0.2, 0.2)), 0.1, 10.0),
        "blocks": normal_values(seeds[3], (COL_DEVS, ROW_DEVS, NB, BS, BS), (4.0 / BS), 0.09375, ((0, 8), (1, 4)), jnp.float32),
        "block_count": draw_block_count(jax.random.fold_in(seeds[7], 71), 0),
        "block_rows": draw_block_rows(jax.random.fold_in(seeds[7], 71), 0),
        "block_cols": draw_block_cols(jax.random.fold_in(seeds[7], 71), 0),
    }


ridge_weight = 0.5


def apply_normal(vector, tiles, global_rows, global_cols, live, scaling):
    picked = vector[global_rows]
    lifted = jnp.einsum("kab,ka->kb", tiles, picked, precision=lax.Precision.HIGHEST) * live[:, None]
    column_total = jax.ops.segment_sum(lifted, global_cols, num_segments=scaling.shape[0])
    weighted = scaling * column_total
    spread = weighted[global_cols]
    contrib = jnp.einsum("kab,kb->ka", tiles, spread, precision=lax.Precision.HIGHEST) * live[:, None]
    summed = jax.ops.segment_sum(contrib, global_rows, num_segments=vector.shape[0])
    return summed + ridge_weight * vector


def reference(right_side, precond, scaling, blocks, block_count, block_rows, block_cols):
    tiles = blocks.reshape((-1, blocks.shape[3], blocks.shape[4]))
    slots = jnp.arange(NB, dtype=jnp.int32)
    live = (slots[None, None, :] < block_count[:, :, None]).astype(jnp.float32).reshape(-1)
    row_base = (jnp.arange(ROW_DEVS, dtype=jnp.int32) * GROUP_ROWS)[None, :, None]
    col_base = (jnp.arange(COL_DEVS, dtype=jnp.int32) * CB_DEV)[:, None, None]
    global_rows = (block_rows + row_base).reshape(-1).astype(jnp.int32)
    global_cols = (block_cols + col_base).reshape(-1).astype(jnp.int32)
    solution_field = jnp.zeros_like(right_side)
    residual = right_side
    precon_res = precond * residual
    direction = precon_res
    gamma = jnp.sum(residual * precon_res)
    for step in range(ITERS):
        image = apply_normal(direction, tiles, global_rows, global_cols, live, scaling)
        alpha = gamma / jnp.sum(direction * image)
        solution_field = solution_field + alpha * direction
        residual = residual - alpha * image
        if step + 1 < ITERS:
            precon_res = precond * residual
            gamma_next = jnp.sum(residual * precon_res)
            direction = precon_res + (gamma_next / gamma) * direction
            gamma = gamma_next
    return solution_field, residual
```

```python
import jax
import jax.numpy as jnp
from jax import lax
from jax.experimental import pallas as pl
from jax.experimental.pallas import tpu as pltpu
from jax.sharding import PartitionSpec as P

ridge_weight = 0.5
LANES = 128
EXTRA = 8
VMEM_LIMIT = 16 << 20
F32 = jnp.float32
BF16 = jnp.bfloat16


def vmem():
    return pl.BlockSpec(memory_space=pltpu.VMEM)


def smem():
    return pl.BlockSpec(memory_space=pltpu.SMEM)


def call(body, name, out_shapes, args, in_specs=None, scratch=(), flops=0, moved=0):
    return pl.pallas_call(
        body,
        name=name,
        out_shape=[pltpu.VMEM(s, d) for s, d in out_shapes],
        in_specs=in_specs or [vmem()] * len(args),
        out_specs=[vmem()] * len(out_shapes),
        scratch_shapes=list(scratch),
        compiler_params=pltpu.CompilerParams(vmem_limit_bytes=VMEM_LIMIT),
        cost_estimate=pl.CostEstimate(flops=flops, bytes_accessed=moved, transcendentals=0),
    )(*args)


def split(x):
    high = x.astype(BF16).astype(F32)
    return jnp.concatenate([high, x - high], axis=0).astype(BF16)


def lane_sum(row):
    return jnp.sum(row, axis=1, keepdims=True)


def row_sum(x):
    return jnp.sum(x, axis=0, keepdims=True)


def block_product(table, vector, high, low, slots):
    placed = jnp.dot(table, split(vector), preferred_element_type=F32).astype(BF16)
    step = placed.shape[0] // slots
    size = vector.shape[1]
    total = jnp.zeros((step, size), F32)
    rest = jnp.zeros((step, size), F32)
    for k in range(slots):
        left = placed[k * step : (k + 1) * step]
        total += jnp.dot(left, high[k * size : (k + 1) * size, :], preferred_element_type=F32)
        rest += jnp.dot(left, low[k * size : (k + 1) * size, :], preferred_element_type=F32)
    total += rest
    half = step // 2
    return total[:half] + total[half:]


def prepare_body(group, cols, tiles, count, rows_of, cols_of, high, low, high_t, low_t, to_cols, to_rows, own, buf, sem):
    slots = buf.shape[0]
    size = buf.shape[1]

    def copy(k):
        return pltpu.make_async_copy(tiles.at[0, 0, k], buf.at[k], sem.at[k])

    @pl.loop(0, slots)
    def _(k):
        copy(k).start()

    def table(targets, sources, target, source, live):
        r = lax.broadcasted_iota(jnp.int32, (2 * targets, 2 * sources), 0)
        q = lax.broadcasted_iota(jnp.int32, (2 * targets, 2 * sources), 1)
        first = (r == target) & (q == source)
        second = (r == targets + target) & (q == sources + source)
        return jnp.where((first | second) & live, 1.0, 0.0).astype(BF16)

    @pl.loop(0, slots)
    def _(k):
        live = k < count[0, 0]
        row, col = rows_of[0, 0, k], cols_of[0, 0, k]
        to_cols[pl.ds(pl.multiple_of(k * 2 * cols, 2 * cols), 2 * cols), :] = table(cols, group, col, row, live)
        to_rows[pl.ds(pl.multiple_of(k * 2 * group, 2 * group), 2 * group), :] = table(group, cols, row, col, live)

    mine = lax.broadcasted_iota(jnp.int32, own.shape, 0) == lax.axis_index("col")
    own[...] = jnp.where(mine, 1.0, 0.0)

    @pl.loop(0, slots)
    def _(k):
        copy(k).wait()
        here = pl.ds(pl.multiple_of(k * size, size), size)
        tile = buf[k]
        part = tile.astype(BF16)
        high[here, :] = part
        low[here, :] = (tile - part.astype(F32)).astype(BF16)
        flip = tile.T
        part = flip.astype(BF16)
        high_t[here, :] = part
        low_t[here, :] = (flip - part.astype(F32)).astype(BF16)


def first_body(slots, gathered, high, low, to_cols, out):
    residual, weights = gathered[:, 0, :], gathered[:, 1, :]
    z = weights * residual
    cols = out.shape[0] - EXTRA
    out[pl.ds(cols, EXTRA), :] = jnp.zeros((EXTRA, out.shape[1]), F32)
    out[pl.ds(cols, 1), :] = row_sum(residual * z)
    out[pl.ds(cols + 1, 1), :] = row_sum(z * z)
    out[pl.ds(0, cols), :] = block_product(to_cols[...], z, high, low, slots)


def second_body(slots, peers, p0, p1, p2, p3, scaling, high_t, low_t, to_rows, total, out):
    summed = (p0[...] + p1[...]) + (p2[...] + p3[...])
    total[...] = summed
    cols = scaling.shape[0]
    lifted = summed[:cols]
    weighted = scaling[...] * lifted
    inner = row_sum(weighted * lifted)
    rows = block_product(to_rows[...], weighted, high_t, low_t, slots)
    group = rows.shape[0]
    for j in range(peers):
        out[j, pl.ds(0, group), :] = rows
        out[j, pl.ds(group, EXTRA), :] = jnp.broadcast_to(inner, (EXTRA, inner.shape[1]))


def third_body(slots, arrived, gathered, total, high, low, to_cols, out, residual_out, alpha_out):
    residual, weights = gathered[:, 0, :], gathered[:, 1, :]
    z = weights * residual
    group = residual.shape[0]
    cols = out.shape[0] - EXTRA
    summed = jnp.sum(arrived[...], axis=0)
    image = summed[:group] + ridge_weight * z
    gamma = lane_sum(total[pl.ds(cols, 1), :])
    curve = lane_sum(summed[group : group + 1]) + ridge_weight * lane_sum(total[pl.ds(cols + 1, 1), :])
    alpha = gamma / curve
    alpha_out[...] = jnp.broadcast_to(alpha, alpha_out.shape)
    later = residual - alpha * image
    residual_out[...] = later
    z1 = weights * later
    out[pl.ds(cols, EXTRA), :] = jnp.zeros((EXTRA, out.shape[1]), F32)
    out[pl.ds(cols, 1), :] = row_sum(later * z1)
    out[pl.ds(cols + 1, 1), :] = row_sum(z1 * z1)
    out[pl.ds(cols + 2, 1), :] = row_sum(z1 * z)
    out[pl.ds(0, cols), :] = block_product(to_cols[...], z1, high, low, slots)


def fourth_body(slots, p0, p1, p2, p3, total, gathered, residual, scaling, high_t, low_t, to_rows, out, direction_out, scalars):
    summed = (p0[...] + p1[...]) + (p2[...] + p3[...])
    cols = scaling.shape[0]
    gamma = lane_sum(total[pl.ds(cols, 1), :])
    norm = lane_sum(total[pl.ds(cols + 1, 1), :])
    later = lane_sum(summed[cols : cols + 1])
    beta = later / gamma
    square = lane_sum(summed[cols + 1 : cols + 2]) + beta * (2.0 * lane_sum(summed[cols + 2 : cols + 3]) + beta * norm)
    lifted = summed[:cols] + beta * total[pl.ds(0, cols), :]
    weighted = scaling[...] * lifted
    inner = row_sum(weighted * lifted)
    rows = block_product(to_rows[...], weighted, high_t, low_t, slots)
    peers, pieces = out.shape[0], rows.shape[1] // LANES
    own = rows.shape[0] // peers
    for h in range(pieces):
        here = slice(h * LANES, (h + 1) * LANES)
        for m in range(own):
            out[:, m * pieces + h, :] = rows.reshape(peers, own, -1)[:, m, here] if own > 1 else rows[:, here]
        out[:, own * pieces + h, :] = jnp.broadcast_to(inner[:, here], (peers, LANES))
    weights = gathered[:, 1, :]
    direction_out[...] = weights * residual[...] + beta * (weights * gathered[:, 0, :])
    scalars[pl.ds(0, 1), :] = jnp.broadcast_to(later, (1, LANES))
    scalars[pl.ds(1, 1), :] = jnp.broadcast_to(square, (1, LANES))


def last_body(arrived, gathered, residual, direction, alpha, scalars, own, solution, residual_out):
    pieces = solution.shape[1] // LANES
    mask = own[:, :1]
    summed = jnp.sum(arrived[...], axis=0)
    image = jnp.concatenate([summed[h : h + 1] for h in range(pieces)], axis=1)
    inner = summed[pieces : pieces + 1]
    for h in range(1, pieces):
        inner += summed[pieces + h : pieces + h + 1]
    curve = lane_sum(inner) + ridge_weight * scalars[1:2, :1]
    step = scalars[0:1, :1] / curve
    first = row_sum(mask * (gathered[:, 0, :] * gathered[:, 1, :]))
    second = row_sum(mask * direction[...])
    before = row_sum(mask * residual[...])
    solution[...] = alpha[:1, :1] * first + step * second
    residual_out[...] = before - step * (image + ridge_weight * second)


def share(value, axis, size):
    moved = [value]
    for s in range(1, size):
        moved.append(lax.ppermute(value, axis, [(i, i ^ s) for i in range(size)]))
    return moved


def local(right_side, precond, scaling, blocks, block_count, block_rows, block_cols):
    peers = lax.axis_size("col")
    groups = lax.axis_size("row")
    slots, size = blocks.shape[2], blocks.shape[3]
    group = right_side.shape[0] * peers
    cols = scaling.shape[0]
    long = slots * size

    both = jnp.stack([right_side, precond], axis=1)
    gathered = lax.all_to_all(
        jnp.broadcast_to(both, (peers, 2, size)), "col", 0, 0, tiled=True
    )
    high, low, high_t, low_t, to_cols, to_rows, own = call(
        lambda *refs: prepare_body(group, cols, *refs),
        "prepare",
        [((long, size), BF16)] * 4
        + [((slots * 2 * cols, 2 * group), BF16), ((slots * 2 * group, 2 * cols), BF16), ((group, LANES), F32)],
        (blocks, block_count, block_rows, block_cols),
        in_specs=[pl.BlockSpec(memory_space=pl.ANY), smem(), smem(), smem()],
        scratch=[pltpu.VMEM((slots, size, size), F32), pltpu.SemaphoreType.DMA((slots,))],
        flops=8 * long * size,
        moved=4 * long * size,
    )
    work = dict(flops=8 * long * size, moved=0)
    (mine,) = call(
        lambda *refs: first_body(slots, *refs),
        "first",
        [((cols + EXTRA, size), F32)],
        (gathered, high, low, to_cols),
        **work,
    )
    total, sent = call(
        lambda *refs: second_body(slots, peers, *refs),
        "second",
        [((cols + EXTRA, size), F32), ((peers, group + EXTRA, size), F32)],
        (*share(mine, "row", groups), scaling, high_t, low_t, to_rows),
        **work,
    )
    arrived = lax.all_to_all(sent, "col", 0, 0, tiled=True)
    mine, residual, alpha = call(
        lambda *refs: third_body(slots, *refs),
        "third",
        [((cols + EXTRA, size), F32), ((group, size), F32), ((1, LANES), F32)],
        (arrived, gathered, total, high, low, to_cols),
        **work,
    )
    pieces = size // LANES
    sent, direction, scalars = call(
        lambda *refs: fourth_body(slots, *refs),
        "fourth",
        [((peers, (right_side.shape[0] + 1) * pieces, LANES), F32), ((group, size), F32), ((2, LANES), F32)],
        (*share(mine, "row", groups), total, gathered, residual, scaling, high_t, low_t, to_rows),
        **work,
    )
    arrived = lax.all_to_all(sent, "col", 0, 0, tiled=True)
    return pl.pallas_call(
        last_body,
        name="last",
        out_shape=[jax.ShapeDtypeStruct(right_side.shape, F32)] * 2,
        in_specs=[vmem()] * 7,
        out_specs=[vmem()] * 2,
        compiler_params=pltpu.CompilerParams(vmem_limit_bytes=VMEM_LIMIT),
    )(arrived, gathered, residual, direction, alpha, scalars, own)


def solution(mesh):
    placed = (
        P(("row", "col"), None),
        P(("row", "col"), None),
        P("col", None),
        P("col", "row", None, None, None),
        P("col", "row"),
        P("col", "row", None),
        P("col", "row", None),
    )
    return jax.shard_map(
        local,
        mesh=mesh,
        in_specs=placed,
        out_specs=(P(("row", "col"), None), P(("row", "col"), None)),
        check_vma=False,
    )
```

```python
import jax
import jax.numpy as jnp
from jax import lax
from jax.experimental import pallas as pl
from jax.experimental.pallas import tpu as pltpu
from jax.sharding import PartitionSpec as P

ridge_weight = 0.5
LANES = 128
EXTRA = 8
VMEM_LIMIT = 16 << 20
F32 = jnp.float32
BF16 = jnp.bfloat16


def vmem():
    return pl.BlockSpec(memory_space=pltpu.VMEM)


def stay(x):
    return pltpu.with_memory_space_constraint(x, pltpu.HBM)


def call(body, name, out_shapes, args, in_specs=None, scratch=(), flops=0, moved=0):
    return pl.pallas_call(
        body,
        name=name,
        out_shape=[pltpu.VMEM(s, d) for s, d in out_shapes],
        in_specs=in_specs or [vmem()] * len(args),
        out_specs=[vmem()] * len(out_shapes),
        scratch_shapes=list(scratch),
        compiler_params=pltpu.CompilerParams(vmem_limit_bytes=VMEM_LIMIT),
        cost_estimate=pl.CostEstimate(flops=flops, bytes_accessed=moved, transcendentals=0),
    )(*args)


def split(x):
    high = x.astype(BF16).astype(F32)
    return jnp.concatenate([high, x - high], axis=0).astype(BF16)


def lane_sum(row):
    return jnp.sum(row, axis=1, keepdims=True)


def row_sum(x):
    return jnp.sum(x, axis=0, keepdims=True)


def pieces_of(x):
    return [x[:, h : h + LANES] for h in range(0, x.shape[1], LANES)]


def fold(row):
    return sum(pieces_of(row)[1:], pieces_of(row)[0])


def put(ref, first, x):
    for piece in pieces_of(x):
        ref[pl.ds(first, piece.shape[0]), 0, :] = piece
        first += piece.shape[0]


def take(x, rows, size):
    return jnp.concatenate([x[h * rows : (h + 1) * rows] for h in range(size // LANES)], axis=1)


def place(table, vector):
    return jnp.dot(table, split(vector), preferred_element_type=F32).astype(BF16)


def join(total):
    half = total.shape[0] // 2
    return total[:half] + total[half:]


def block_product(table, vector, high, low, slots, flip):
    placed = place(table, vector)
    step = placed.shape[0] // slots
    size = vector.shape[1]
    contract = (((1,), (1 if flip else 0,)), ((), ()))
    total = jnp.zeros((step, size), F32)
    rest = jnp.zeros((step, size), F32)
    for k in range(slots):
        left = placed[k * step : (k + 1) * step]
        here = slice(k * size, (k + 1) * size)
        total += lax.dot_general(left, high[here, :], contract, preferred_element_type=F32)
        rest += lax.dot_general(left, low[here, :], contract, preferred_element_type=F32)
    return join(total + rest)


def start_body(group, cols, slots, *refs):
    sources, (sent, to_cols, to_rows, own), held, sem = refs[:5], refs[5:9], refs[9:14], refs[14]
    copies = [pltpu.make_async_copy(a, b, sem.at[i]) for i, (a, b) in enumerate(zip(sources, held))]
    for copy in copies:
        copy.start()
    mine = lax.broadcasted_iota(jnp.int32, own.shape, 0) == lax.axis_index("col")
    own[...] = jnp.where(mine, 1.0, 0.0)
    for copy in copies:
        copy.wait()
    side, weights, count, rows_of, cols_of = held
    both = jnp.concatenate([side[...], weights[...]], axis=0)
    sent[...] = jnp.broadcast_to(both[None], sent.shape)

    def table(targets, sources, target, source, live):
        r = lax.broadcasted_iota(jnp.int32, (2 * targets, 2 * sources), 0)
        q = lax.broadcasted_iota(jnp.int32, (2 * targets, 2 * sources), 1)
        first = (r == target) & (q == source)
        second = (r == targets + target) & (q == sources + source)
        return jnp.where((first | second) & live, 1.0, 0.0).astype(BF16)

    for k in range(slots):
        live = k < count[0, 0]
        row, col = rows_of[0, 0, k], cols_of[0, 0, k]
        to_cols[pl.ds(k * 2 * cols, 2 * cols), :] = table(cols, group, col, row, live)
        to_rows[pl.ds(k * 2 * group, 2 * group), :] = table(group, cols, row, col, live)


def first_body(slots, cols, gathered, tiles, to_cols, out, high, low):
    residual, weights = gathered[:, 0, :], gathered[:, 1, :]
    z = weights * residual
    size = z.shape[1]
    placed = place(to_cols[...], z)
    step = 2 * cols
    total = jnp.zeros((step, size), F32)
    rest = jnp.zeros((step, size), F32)
    for k in range(slots):
        left = placed[k * step : (k + 1) * step]
        tile = tiles[0, 0, k]
        upper = tile.astype(BF16)
        lower = (tile - upper.astype(F32)).astype(BF16)
        high[pl.ds(k * size, size), :] = upper
        low[pl.ds(k * size, size), :] = lower
        total += jnp.dot(left, upper, preferred_element_type=F32)
        rest += jnp.dot(left, lower, preferred_element_type=F32)
    put(out, 0, join(total + rest))
    count = cols * (size // LANES)
    put(out, count, fold(row_sum(residual * z)))
    put(out, count + 1, fold(row_sum(z * z)))


def gather4(refs):
    a, b, c, d = [r[:, 0, :] for r in refs]
    return (a + b) + (c + d)


def second_body(slots, peers, p0, p1, p2, p3, scaling, high, low, to_rows, total, out):
    summed = gather4((p0, p1, p2, p3))
    total[...] = summed
    cols, size = scaling.shape
    lifted = take(summed, cols, size)
    weighted = scaling[...] * lifted
    inner = fold(row_sum(weighted * lifted))
    rows = block_product(to_rows[...], weighted, high, low, slots, True)
    length = out.shape[0] // peers
    for j in range(peers):
        put(out, j * length, rows)
        put(out, (j + 1) * length - 1, inner)


def third_body(slots, cols, arrived, gathered, total, high, low, to_cols, out, residual_out, alpha_out):
    residual, weights = gathered[:, 0, :], gathered[:, 1, :]
    z = weights * residual
    group, size = residual.shape
    length = group * (size // LANES) + 1
    peers = arrived.shape[0] // length
    summed = arrived[pl.ds(0, length), 0, :]
    for j in range(1, peers):
        summed += arrived[pl.ds(j * length, length), 0, :]
    image = take(summed, group, size) + ridge_weight * z
    count = cols * (size // LANES)
    gamma = lane_sum(total[pl.ds(count, 1), :])
    curve = lane_sum(summed[length - 1 : length] + ridge_weight * total[pl.ds(count + 1, 1), :])
    alpha = gamma / curve
    alpha_out[...] = jnp.broadcast_to(alpha, alpha_out.shape)
    later = residual - alpha * image
    residual_out[...] = later
    z1 = weights * later
    put(out, count, fold(row_sum(later * z1)))
    put(out, count + 1, fold(row_sum(z1 * z1)))
    put(out, count + 2, fold(row_sum(z1 * z)))
    put(out, 0, block_product(to_cols[...], z1, high, low, slots, False))


def fourth_body(slots, p0, p1, p2, p3, total, gathered, residual, scaling, high, low, to_rows, out, direction_out, scalars):
    summed = gather4((p0, p1, p2, p3))
    cols, size = scaling.shape
    count = cols * (size // LANES)
    gamma = lane_sum(total[pl.ds(count, 1), :])
    norm = lane_sum(total[pl.ds(count + 1, 1), :])
    later = lane_sum(summed[count : count + 1])
    beta = later / gamma
    square = lane_sum(summed[count + 1 : count + 2]) + beta * (2.0 * lane_sum(summed[count + 2 : count + 3]) + beta * norm)
    lifted = take(summed, cols, size) + beta * take(total[...], cols, size)
    weighted = scaling[...] * lifted
    inner = fold(row_sum(weighted * lifted))
    rows = block_product(to_rows[...], weighted, high, low, slots, True)
    peers = out.shape[0]
    for h, piece in enumerate(pieces_of(rows)):
        out[:, h, :] = piece
    out[:, size // LANES, :] = jnp.broadcast_to(inner, (peers, LANES))
    weights = gathered[:, 1, :]
    direction_out[...] = weights * residual[...] + beta * (weights * gathered[:, 0, :])
    scalars[pl.ds(0, 1), :] = jnp.broadcast_to(later, (1, LANES))
    scalars[pl.ds(1, 1), :] = jnp.broadcast_to(square, (1, LANES))


def last_body(arrived, gathered, residual, direction, alpha, scalars, own, solution, residual_out):
    size = solution.shape[1]
    mask = own[:, :1]
    summed = jnp.sum(arrived[...], axis=0)
    image = take(summed, 1, size)
    curve = lane_sum(summed[size // LANES : size // LANES + 1]) + ridge_weight * scalars[1:2, :1]
    step = scalars[0:1, :1] / curve
    first = row_sum(mask * (gathered[:, 0, :] * gathered[:, 1, :]))
    second = row_sum(mask * direction[...])
    before = row_sum(mask * residual[...])
    solution[...] = alpha[:1, :1] * first + step * second
    residual_out[...] = before - step * (image + ridge_weight * second)


def share(value, axis, size):
    moved = [value]
    for s in range(1, size):
        moved.append(lax.ppermute(value, axis, [(i, i ^ s) for i in range(size)]))
    return moved


def local(right_side, precond, scaling, blocks, block_count, block_rows, block_cols):
    peers = lax.axis_size("col")
    groups = lax.axis_size("row")
    slots, size = blocks.shape[2], blocks.shape[3]
    own_rows = right_side.shape[0]
    assert own_rows == 1 and groups == 4
    group = own_rows * peers
    cols = scaling.shape[0]
    pieces = size // LANES
    long = slots * size
    work = dict(flops=8 * long * size, moved=0)

    sent, to_cols, to_rows, own = call(
        lambda *refs: start_body(group, cols, slots, *refs),
        "start",
        [
            ((peers, 2, size), F32),
            ((slots * 2 * cols, 2 * group), BF16),
            ((slots * 2 * group, 2 * cols), BF16),
            ((group, LANES), F32),
        ],
        (stay(right_side), stay(precond), block_count, stay(block_rows), stay(block_cols)),
        in_specs=[pl.BlockSpec(memory_space=pl.ANY)] * 5,
        scratch=[
            pltpu.VMEM(right_side.shape, F32),
            pltpu.VMEM(precond.shape, F32),
            pltpu.SMEM(block_count.shape, jnp.int32),
            pltpu.SMEM(block_rows.shape, jnp.int32),
            pltpu.SMEM(block_cols.shape, jnp.int32),
            pltpu.SemaphoreType.DMA((5,)),
        ],
        moved=100 << 20,
    )
    held_blocks = lax.ppermute(blocks, "col", [(i, i) for i in range(peers)])
    gathered = lax.all_to_all(sent, "col", 0, 0, tiled=True)
    mine, high, low = call(
        lambda *refs: first_body(slots, cols, *refs),
        "first",
        [((cols * pieces + 2, 1, LANES), F32), ((long, size), BF16), ((long, size), BF16)],
        (gathered, held_blocks, to_cols),
        **work,
    )
    length = group * pieces + 1
    total, sent = call(
        lambda *refs: second_body(slots, peers, *refs),
        "second",
        [((cols * pieces + 2, LANES), F32), ((peers * length, 1, LANES), F32)],
        (*share(mine, "row", groups), scaling, high, low, to_rows),
        **work,
    )
    arrived = lax.all_to_all(sent, "col", 0, 0, tiled=True)
    mine, residual, alpha = call(
        lambda *refs: third_body(slots, cols, *refs),
        "third",
        [((cols * pieces + 3, 1, LANES), F32), ((group, size), F32), ((1, LANES), F32)],
        (arrived, gathered, total, high, low, to_cols),
        **work,
    )
    sent, direction, scalars = call(
        lambda *refs: fourth_body(slots, *refs),
        "fourth",
        [((peers, pieces + 1, LANES), F32), ((group, size), F32), ((2, LANES), F32)],
        (*share(mine, "row", groups), total, gathered, residual, scaling, high, low, to_rows),
        **work,
    )
    arrived = lax.all_to_all(sent, "col", 0, 0, tiled=True)
    return pl.pallas_call(
        last_body,
        name="last",
        out_shape=[jax.ShapeDtypeStruct(right_side.shape, F32)] * 2,
        in_specs=[vmem()] * 7,
        out_specs=[vmem()] * 2,
        compiler_params=pltpu.CompilerParams(vmem_limit_bytes=VMEM_LIMIT),
    )(arrived, gathered, residual, direction, alpha, scalars, own)


def solution(mesh):
    placed = (
        P(("row", "col"), None),
        P(("row", "col"), None),
        P("col", None),
        P("col", "row", None, None, None),
        P("col", "row"),
        P("col", "row", None),
        P("col", "row", None),
    )
    return jax.shard_map(
        local,
        mesh=mesh,
        in_specs=placed,
        out_specs=(P(("row", "col"), None), P(("row", "col"), None)),
        check_vma=False,
    )
```

```python
import jax
import jax.numpy as jnp
from jax import lax
from jax.experimental import pallas as pl
from jax.experimental.pallas import tpu as pltpu
from jax.sharding import PartitionSpec as P

ridge_weight = 0.5
LANES = 128
EXTRA = 8
VMEM_LIMIT = 16 << 20
F32 = jnp.float32
BF16 = jnp.bfloat16


def vmem():
    return pl.BlockSpec(memory_space=pltpu.VMEM)


def stay(x):
    return pltpu.with_memory_space_constraint(x, pltpu.HBM)


def call(body, name, out_shapes, args, in_specs=None, scratch=(), flops=0, moved=0):
    return pl.pallas_call(
        body,
        name=name,
        out_shape=[pltpu.VMEM(s, d) for s, d in out_shapes],
        in_specs=in_specs or [vmem()] * len(args),
        out_specs=[vmem()] * len(out_shapes),
        scratch_shapes=list(scratch),
        compiler_params=pltpu.CompilerParams(vmem_limit_bytes=VMEM_LIMIT),
        cost_estimate=pl.CostEstimate(flops=flops, bytes_accessed=moved, transcendentals=0),
    )(*args)


def split(x):
    high = x.astype(BF16).astype(F32)
    return jnp.concatenate([high, x - high], axis=0).astype(BF16)


def lane_sum(row):
    return jnp.sum(row, axis=1, keepdims=True)


def row_sum(x):
    return jnp.sum(x, axis=0, keepdims=True)


def pieces_of(x):
    return [x[:, h : h + LANES] for h in range(0, x.shape[1], LANES)]


def fold(row):
    return sum(pieces_of(row)[1:], pieces_of(row)[0])


def put(ref, first, x):
    for piece in pieces_of(x):
        ref[pl.ds(first, piece.shape[0]), 0, :] = piece
        first += piece.shape[0]


def take(x, rows, size):
    return jnp.concatenate([x[h * rows : (h + 1) * rows] for h in range(size // LANES)], axis=1)


def place(table, vector):
    return jnp.dot(table, split(vector), preferred_element_type=F32).astype(BF16)


def join(total):
    half = total.shape[0] // 2
    return total[:half] + total[half:]


def block_product(table, vector, high, low, slots, flip):
    placed = place(table, vector)
    step = placed.shape[0] // slots
    size = vector.shape[1]
    contract = (((1,), (1 if flip else 0,)), ((), ()))
    total = jnp.zeros((step, size), F32)
    rest = jnp.zeros((step, size), F32)
    for k in range(slots):
        left = placed[k * step : (k + 1) * step]
        here = slice(k * size, (k + 1) * size)
        total += lax.dot_general(left, high[here, :], contract, preferred_element_type=F32)
        rest += lax.dot_general(left, low[here, :], contract, preferred_element_type=F32)
    return join(total + rest)


def start_body(group, cols, slots, *refs):
    sources, (sent, to_cols, to_rows, own), held, sem = refs[:5], refs[5:9], refs[9:14], refs[14]
    copies = [pltpu.make_async_copy(a, b, sem.at[i]) for i, (a, b) in enumerate(zip(sources, held))]
    for copy in copies:
        copy.start()
    mine = lax.broadcasted_iota(jnp.int32, own.shape, 0) == lax.axis_index("col")
    own[...] = jnp.where(mine, 1.0, 0.0)
    for copy in copies:
        copy.wait()
    side, weights, count, rows_of, cols_of = held
    both = jnp.concatenate([side[...], weights[...]], axis=0)
    sent[...] = jnp.broadcast_to(both[None], sent.shape)

    def table(targets, sources, target, source, live):
        r = lax.broadcasted_iota(jnp.int32, (2 * targets, 2 * sources), 0)
        q = lax.broadcasted_iota(jnp.int32, (2 * targets, 2 * sources), 1)
        first = (r == target) & (q == source)
        second = (r == targets + target) & (q == sources + source)
        return jnp.where((first | second) & live, 1.0, 0.0).astype(BF16)

    for k in range(slots):
        live = k < count[0, 0]
        row, col = rows_of[0, 0, k], cols_of[0, 0, k]
        to_cols[pl.ds(k * 2 * cols, 2 * cols), :] = table(cols, group, col, row, live)
        to_rows[pl.ds(k * 2 * group, 2 * group), :] = table(group, cols, row, col, live)


def first_body(slots, cols, gathered, tiles, to_cols, out, high, low, high_t, low_t):
    residual, weights = gathered[:, 0, :], gathered[:, 1, :]
    z = weights * residual
    size = z.shape[1]
    placed = place(to_cols[...], z)
    step = 2 * cols
    total = jnp.zeros((step, size), F32)
    rest = jnp.zeros((step, size), F32)
    for k in range(slots):
        left = placed[k * step : (k + 1) * step]
        tile = tiles[0, 0, k]
        upper = tile.astype(BF16)
        lower = (tile - upper.astype(F32)).astype(BF16)
        high[pl.ds(k * size, size), :] = upper
        low[pl.ds(k * size, size), :] = lower
        high_t[pl.ds(k * size, size), :] = upper.T
        low_t[pl.ds(k * size, size), :] = lower.T
        total += jnp.dot(left, upper, preferred_element_type=F32)
        rest += jnp.dot(left, lower, preferred_element_type=F32)
    put(out, 0, join(total + rest))
    count = cols * (size // LANES)
    put(out, count, fold(row_sum(residual * z)))
    put(out, count + 1, fold(row_sum(z * z)))


def gather4(refs):
    a, b, c, d = [r[:, 0, :] for r in refs]
    return (a + b) + (c + d)


def second_body(slots, peers, p0, p1, p2, p3, scaling, high, low, to_rows, total, out):
    summed = gather4((p0, p1, p2, p3))
    total[...] = summed
    cols, size = scaling.shape
    lifted = take(summed, cols, size)
    weighted = scaling[...] * lifted
    inner = fold(row_sum(weighted * lifted))
    rows = block_product(to_rows[...], weighted, high, low, slots, False)
    length = out.shape[0] // peers
    for j in range(peers):
        put(out, j * length, rows)
        put(out, (j + 1) * length - 1, inner)


def third_body(slots, cols, arrived, gathered, total, high, low, to_cols, out, residual_out, alpha_out):
    residual, weights = gathered[:, 0, :], gathered[:, 1, :]
    z = weights * residual
    group, size = residual.shape
    length = group * (size // LANES) + 1
    peers = arrived.shape[0] // length
    summed = arrived[pl.ds(0, length), 0, :]
    for j in range(1, peers):
        summed += arrived[pl.ds(j * length, length), 0, :]
    image = take(summed, group, size) + ridge_weight * z
    count = cols * (size // LANES)
    gamma = lane_sum(total[pl.ds(count, 1), :])
    curve = lane_sum(summed[length - 1 : length] + ridge_weight * total[pl.ds(count + 1, 1), :])
    alpha = gamma / curve
    alpha_out[...] = jnp.broadcast_to(alpha, alpha_out.shape)
    later = residual - alpha * image
    residual_out[...] = later
    z1 = weights * later
    put(out, count, fold(row_sum(later * z1)))
    put(out, count + 1, fold(row_sum(z1 * z1)))
    put(out, count + 2, fold(row_sum(z1 * z)))
    put(out, 0, block_product(to_cols[...], z1, high, low, slots, False))


def fourth_body(slots, p0, p1, p2, p3, total, gathered, residual, scaling, high, low, to_rows, out, direction_out, scalars):
    summed = gather4((p0, p1, p2, p3))
    cols, size = scaling.shape
    count = cols * (size // LANES)
    gamma = lane_sum(total[pl.ds(count, 1), :])
    norm = lane_sum(total[pl.ds(count + 1, 1), :])
    later = lane_sum(summed[count : count + 1])
    beta = later / gamma
    square = lane_sum(summed[count + 1 : count + 2]) + beta * (2.0 * lane_sum(summed[count + 2 : count + 3]) + beta * norm)
    lifted = take(summed, cols, size) + beta * take(total[...], cols, size)
    weighted = scaling[...] * lifted
    inner = fold(row_sum(weighted * lifted))
    rows = block_product(to_rows[...], weighted, high, low, slots, False)
    peers = out.shape[0]
    for h, piece in enumerate(pieces_of(rows)):
        out[:, h, :] = piece
    out[:, size // LANES, :] = jnp.broadcast_to(inner, (peers, LANES))
    weights = gathered[:, 1, :]
    direction_out[...] = weights * residual[...] + beta * (weights * gathered[:, 0, :])
    scalars[pl.ds(0, 1), :] = jnp.broadcast_to(later, (1, LANES))
    scalars[pl.ds(1, 1), :] = jnp.broadcast_to(square, (1, LANES))


def last_body(arrived, gathered, residual, direction, alpha, scalars, own, solution, residual_out):
    size = solution.shape[1]
    mask = own[:, :1]
    summed = jnp.sum(arrived[...], axis=0)
    image = take(summed, 1, size)
    curve = lane_sum(summed[size // LANES : size // LANES + 1]) + ridge_weight * scalars[1:2, :1]
    step = scalars[0:1, :1] / curve
    first = row_sum(mask * (gathered[:, 0, :] * gathered[:, 1, :]))
    second = row_sum(mask * direction[...])
    before = row_sum(mask * residual[...])
    solution[...] = alpha[:1, :1] * first + step * second
    residual_out[...] = before - step * (image + ridge_weight * second)


def share(value, axis, size):
    moved = [value]
    for s in range(1, size):
        moved.append(lax.ppermute(value, axis, [(i, i ^ s) for i in range(size)]))
    return moved


def local(right_side, precond, scaling, blocks, block_count, block_rows, block_cols):
    peers = lax.axis_size("col")
    groups = lax.axis_size("row")
    slots, size = blocks.shape[2], blocks.shape[3]
    own_rows = right_side.shape[0]
    assert own_rows == 1 and groups == 4
    group = own_rows * peers
    cols = scaling.shape[0]
    pieces = size // LANES
    long = slots * size
    work = dict(flops=8 * long * size, moved=0)

    sent, to_cols, to_rows, own = call(
        lambda *refs: start_body(group, cols, slots, *refs),
        "start",
        [
            ((peers, 2, size), F32),
            ((slots * 2 * cols, 2 * group), BF16),
            ((slots * 2 * group, 2 * cols), BF16),
            ((group, LANES), F32),
        ],
        (stay(right_side), stay(precond), block_count, stay(block_rows), stay(block_cols)),
        in_specs=[pl.BlockSpec(memory_space=pl.ANY)] * 5,
        scratch=[
            pltpu.VMEM(right_side.shape, F32),
            pltpu.VMEM(precond.shape, F32),
            pltpu.SMEM(block_count.shape, jnp.int32),
            pltpu.SMEM(block_rows.shape, jnp.int32),
            pltpu.SMEM(block_cols.shape, jnp.int32),
            pltpu.SemaphoreType.DMA((5,)),
        ],
        flops=1 << 34,
        moved=100 << 20,
    )
    gathered = lax.all_to_all(sent, "col", 0, 0, tiled=True)
    mine, high, low, high_t, low_t = call(
        lambda *refs: first_body(slots, cols, *refs),
        "first",
        [((cols * pieces + 2, 1, LANES), F32)] + [((long, size), BF16)] * 4,
        (gathered, blocks, to_cols),
        **work,
    )
    length = group * pieces + 1
    total, sent = call(
        lambda *refs: second_body(slots, peers, *refs),
        "second",
        [((cols * pieces + 2, LANES), F32), ((peers * length, 1, LANES), F32)],
        (*share(mine, "row", groups), scaling, high_t, low_t, to_rows),
        **work,
    )
    arrived = lax.all_to_all(sent, "col", 0, 0, tiled=True)
    mine, residual, alpha = call(
        lambda *refs: third_body(slots, cols, *refs),
        "third",
        [((cols * pieces + 3, 1, LANES), F32), ((group, size), F32), ((1, LANES), F32)],
        (arrived, gathered, total, high, low, to_cols),
        **work,
    )
    sent, direction, scalars = call(
        lambda *refs: fourth_body(slots, *refs),
        "fourth",
        [((peers, pieces + 1, LANES), F32), ((group, size), F32), ((2, LANES), F32)],
        (*share(mine, "row", groups), total, gathered, residual, scaling, high_t, low_t, to_rows),
        **work,
    )
    arrived = lax.all_to_all(sent, "col", 0, 0, tiled=True)
    return pl.pallas_call(
        last_body,
        name="last",
        out_shape=[jax.ShapeDtypeStruct(right_side.shape, F32)] * 2,
        in_specs=[vmem()] * 7,
        out_specs=[vmem()] * 2,
        compiler_params=pltpu.CompilerParams(vmem_limit_bytes=VMEM_LIMIT),
    )(arrived, gathered, residual, direction, alpha, scalars, own)


def solution(mesh):
    placed = (
        P(("row", "col"), None),
        P(("row", "col"), None),
        P("col", None),
        P("col", "row", None, None, None),
        P("col", "row"),
        P("col", "row", None),
        P("col", "row", None),
    )
    return jax.shard_map(
        local,
        mesh=mesh,
        in_specs=placed,
        out_specs=(P(("row", "col"), None), P(("row", "col"), None)),
        check_vma=False,
    )
```

```python
import jax
import jax.numpy as jnp
from jax import lax
from jax.experimental import pallas as pl
from jax.experimental.pallas import tpu as pltpu
from jax.sharding import PartitionSpec as P

ridge_weight = 0.5
LANES = 128
FLIP = 1 << 30
VMEM_LIMIT = 16 << 20
F32 = jnp.float32
BF16 = jnp.bfloat16


def vmem():
    return pl.BlockSpec(memory_space=pltpu.VMEM)


def stay(x):
    return pltpu.with_memory_space_constraint(x, pltpu.HBM)


def call(body, name, out_shapes, args, in_specs=None, scratch=(), flops=0, moved=0):
    return pl.pallas_call(
        body,
        name=name,
        out_shape=[pltpu.VMEM(s, d) for s, d in out_shapes],
        in_specs=in_specs or [vmem()] * len(args),
        out_specs=[vmem()] * len(out_shapes),
        scratch_shapes=list(scratch),
        compiler_params=pltpu.CompilerParams(vmem_limit_bytes=VMEM_LIMIT),
        cost_estimate=pl.CostEstimate(flops=flops, bytes_accessed=moved, transcendentals=0),
    )(*args)


def split3(x):
    high = x.astype(BF16).astype(F32)
    rest = x - high
    middle = rest.astype(BF16).astype(F32)
    return jnp.concatenate([high, middle, rest - middle], axis=0).astype(BF16)


def lane_sum(row):
    return jnp.sum(row, axis=1, keepdims=True)


def row_sum(x):
    return jnp.sum(x, axis=0, keepdims=True)


def pieces_of(x):
    return [x[:, h : h + LANES] for h in range(0, x.shape[1], LANES)]


def fold(row):
    return sum(pieces_of(row)[1:], pieces_of(row)[0])


def put(ref, first, x):
    for piece in pieces_of(x):
        ref[pl.ds(first, piece.shape[0]), 0, :] = piece
        first += piece.shape[0]


def take(x, rows, size):
    return jnp.concatenate([x[h * rows : (h + 1) * rows] for h in range(size // LANES)], axis=1)


def block_product(spread, gather, vector, tiles, slots):
    terms = split3(vector)
    size = vector.shape[1]
    parts = []
    for k in range(0, slots, 2):
        table = spread[:, k * LANES : (k + 2) * LANES]
        wide = lax.dot_general(terms, table, (((0,), (0,)), ((), ())), preferred_element_type=F32)
        for m in range(2):
            here = wide[:, m * LANES : (m + 1) * LANES]
            row = []
            for h in range(0, size, LANES):
                product = tiles[k + m, :, h : h + LANES] * here
                row.append(jnp.sum(product.reshape(size // 8, 8, LANES), axis=0))
            parts.append(jnp.concatenate(row, axis=1))
    parts = jnp.concatenate(parts, axis=0)
    count = parts.shape[0]
    terms = split3(parts)
    total = jnp.dot(gather[...], terms[:count], preferred_element_type=F32)
    total += jnp.dot(gather[...], terms[count : 2 * count], preferred_element_type=F32)
    return total + jnp.dot(gather[...], terms[2 * count :], preferred_element_type=F32)


def flip_body(tiles, out):
    for k in range(out.shape[0]):
        out[k] = tiles[0, 0, k].T


def start_body(group, cols, slots, *refs):
    sources, (sent, spread_rows, spread_cols, gather_rows, gather_cols, own), held, sem = refs[:5], refs[5:11], refs[11:16], refs[16]
    copies = [pltpu.make_async_copy(a, b, sem.at[i]) for i, (a, b) in enumerate(zip(sources, held))]
    for copy in copies:
        copy.start()
    mine = lax.broadcasted_iota(jnp.int32, own.shape, 0) == lax.axis_index("col")
    own[...] = jnp.where(mine, 1.0, 0.0)
    for copy in copies:
        copy.wait()
    side, weights, count, rows_of, cols_of = held
    both = jnp.concatenate([side[...], weights[...]], axis=0)
    sent[...] = jnp.broadcast_to(both[None], sent.shape)

    def tables(spread, gather, extent, index):
        term = lax.broadcasted_iota(jnp.int32, (extent, LANES), 0)
        slot = lax.broadcasted_iota(jnp.int32, gather.shape, 1) // 8
        at = lax.broadcasted_iota(jnp.int32, gather.shape, 0)
        target = jnp.full(gather.shape, -1, jnp.int32)
        for k in range(slots):
            source = jnp.where(k < count[0, 0], index[0, 0, k], -1)
            one = jnp.where(term == source, 1.0, 0.0)
            spread[:, pl.ds(k * LANES, LANES)] = jnp.concatenate([one] * 3, axis=0).astype(BF16)
            target = jnp.where(slot == k, index[0, 0, k], target)
        gather[...] = jnp.where(at == target, 1.0, 0.0).astype(BF16)

    tables(spread_rows, gather_rows, group, rows_of)
    tables(spread_cols, gather_cols, cols, cols_of)


def first_body(slots, cols, gathered, tiles, spread, gather, out):
    residual, weights = gathered[:, 0, :], gathered[:, 1, :]
    z = weights * residual
    size = z.shape[1]
    put(out, 0, block_product(spread, gather, z, tiles.at[0, 0], slots))
    count = cols * (size // LANES)
    put(out, count, fold(row_sum(residual * z)))
    put(out, count + 1, fold(row_sum(z * z)))


def gather4(refs):
    a, b, c, d = [r[:, 0, :] for r in refs]
    return (a + b) + (c + d)


def second_body(slots, peers, p0, p1, p2, p3, scaling, flipped, spread, gather, total, out):
    summed = gather4((p0, p1, p2, p3))
    total[...] = summed
    cols, size = scaling.shape
    lifted = take(summed, cols, size)
    weighted = scaling[...] * lifted
    inner = fold(row_sum(weighted * lifted))
    rows = block_product(spread, gather, weighted, flipped, slots)
    length = out.shape[0] // peers
    for j in range(peers):
        put(out, j * length, rows)
        put(out, (j + 1) * length - 1, inner)


def third_body(slots, cols, arrived, gathered, total, tiles, spread, gather, out, residual_out, alpha_out):
    residual, weights = gathered[:, 0, :], gathered[:, 1, :]
    z = weights * residual
    group, size = residual.shape
    length = group * (size // LANES) + 1
    peers = arrived.shape[0] // length
    summed = arrived[pl.ds(0, length), 0, :]
    for j in range(1, peers):
        summed += arrived[pl.ds(j * length, length), 0, :]
    image = take(summed, group, size) + ridge_weight * z
    count = cols * (size // LANES)
    gamma = lane_sum(total[pl.ds(count, 1), :])
    curve = lane_sum(summed[length - 1 : length] + ridge_weight * total[pl.ds(count + 1, 1), :])
    alpha = gamma / curve
    alpha_out[...] = jnp.broadcast_to(alpha, alpha_out.shape)
    later = residual - alpha * image
    residual_out[...] = later
    z1 = weights * later
    put(out, count, fold(row_sum(later * z1)))
    put(out, count + 1, fold(row_sum(z1 * z1)))
    put(out, count + 2, fold(row_sum(z1 * z)))
    put(out, 0, block_product(spread, gather, z1, tiles.at[0, 0], slots))


def fourth_body(slots, p0, p1, p2, p3, total, gathered, residual, scaling, flipped, spread, gather, out, direction_out, scalars):
    summed = gather4((p0, p1, p2, p3))
    cols, size = scaling.shape
    count = cols * (size // LANES)
    gamma = lane_sum(total[pl.ds(count, 1), :])
    norm = lane_sum(total[pl.ds(count + 1, 1), :])
    later = lane_sum(summed[count : count + 1])
    beta = later / gamma
    square = lane_sum(summed[count + 1 : count + 2]) + beta * (2.0 * lane_sum(summed[count + 2 : count + 3]) + beta * norm)
    lifted = take(summed, cols, size) + beta * take(total[...], cols, size)
    weighted = scaling[...] * lifted
    inner = fold(row_sum(weighted * lifted))
    rows = block_product(spread, gather, weighted, flipped, slots)
    peers = out.shape[0]
    for h, piece in enumerate(pieces_of(rows)):
        out[:, h, :] = piece
    out[:, size // LANES, :] = jnp.broadcast_to(inner, (peers, LANES))
    weights = gathered[:, 1, :]
    direction_out[...] = weights * residual[...] + beta * (weights * gathered[:, 0, :])
    scalars[pl.ds(0, 1), :] = jnp.broadcast_to(later, (1, LANES))
    scalars[pl.ds(1, 1), :] = jnp.broadcast_to(square, (1, LANES))


def last_body(arrived, gathered, residual, direction, alpha, scalars, own, solution, residual_out):
    size = solution.shape[1]
    mask = own[:, :1]
    summed = jnp.sum(arrived[...], axis=0)
    image = take(summed, 1, size)
    curve = lane_sum(summed[size // LANES : size // LANES + 1]) + ridge_weight * scalars[1:2, :1]
    step = scalars[0:1, :1] / curve
    first = row_sum(mask * (gathered[:, 0, :] * gathered[:, 1, :]))
    second = row_sum(mask * direction[...])
    before = row_sum(mask * residual[...])
    solution[...] = alpha[:1, :1] * first + step * second
    residual_out[...] = before - step * (image + ridge_weight * second)


def share(value, axis, size):
    moved = [value]
    for s in range(1, size):
        moved.append(lax.ppermute(value, axis, [(i, i ^ s) for i in range(size)]))
    return moved


def local(right_side, precond, scaling, blocks, block_count, block_rows, block_cols):
    peers = lax.axis_size("col")
    groups = lax.axis_size("row")
    slots, size = blocks.shape[2], blocks.shape[3]
    own_rows = right_side.shape[0]
    assert own_rows == 1 and groups == 4
    group = own_rows * peers
    cols = scaling.shape[0]
    pieces = size // LANES
    long = slots * size
    work = dict(flops=8 * long * size, moved=0)

    sent, spread_rows, spread_cols, gather_rows, gather_cols, own = call(
        lambda *refs: start_body(group, cols, slots, *refs),
        "start",
        [
            ((peers, 2, size), F32),
            ((3 * group, slots * LANES), BF16),
            ((3 * cols, slots * LANES), BF16),
            ((group, slots * 8), BF16),
            ((cols, slots * 8), BF16),
            ((group, LANES), F32),
        ],
        (stay(right_side), stay(precond), block_count, stay(block_rows), stay(block_cols)),
        in_specs=[pl.BlockSpec(memory_space=pl.ANY)] * 5,
        scratch=[
            pltpu.VMEM(right_side.shape, F32),
            pltpu.VMEM(precond.shape, F32),
            pltpu.SMEM(block_count.shape, jnp.int32),
            pltpu.SMEM(block_rows.shape, jnp.int32),
            pltpu.SMEM(block_cols.shape, jnp.int32),
            pltpu.SemaphoreType.DMA((5,)),
        ],
        flops=1 << 34,
        moved=100 << 20,
    )
    gathered = lax.all_to_all(sent, "col", 0, 0, tiled=True)
    (mine,) = call(
        lambda *refs: first_body(slots, cols, *refs),
        "first",
        [((cols * pieces + 2, 1, LANES), F32)],
        (gathered, blocks, spread_rows, gather_cols),
        **work,
    )
    (flipped,) = call(flip_body, "flip", [((slots, size, size), F32)], (blocks,), flops=FLIP)
    length = group * pieces + 1
    total, sent = call(
        lambda *refs: second_body(slots, peers, *refs),
        "second",
        [((cols * pieces + 2, LANES), F32), ((peers * length, 1, LANES), F32)],
        (*share(mine, "row", groups), scaling, flipped, spread_cols, gather_rows),
        **work,
    )
    arrived = lax.all_to_all(sent, "col", 0, 0, tiled=True)
    mine, residual, alpha = call(
        lambda *refs: third_body(slots, cols, *refs),
        "third",
        [((cols * pieces + 3, 1, LANES), F32), ((group, size), F32), ((1, LANES), F32)],
        (arrived, gathered, total, blocks, spread_rows, gather_cols),
        **work,
    )
    sent, direction, scalars = call(
        lambda *refs: fourth_body(slots, *refs),
        "fourth",
        [((peers, pieces + 1, LANES), F32), ((group, size), F32), ((2, LANES), F32)],
        (*share(mine, "row", groups), total, gathered, residual, scaling, flipped, spread_cols, gather_rows),
        **work,
    )
    arrived = lax.all_to_all(sent, "col", 0, 0, tiled=True)
    return pl.pallas_call(
        last_body,
        name="last",
        out_shape=[jax.ShapeDtypeStruct(right_side.shape, F32)] * 2,
        in_specs=[vmem()] * 7,
        out_specs=[vmem()] * 2,
        compiler_params=pltpu.CompilerParams(vmem_limit_bytes=VMEM_LIMIT),
    )(arrived, gathered, residual, direction, alpha, scalars, own)


def solution(mesh):
    placed = (
        P(("row", "col"), None),
        P(("row", "col"), None),
        P("col", None),
        P("col", "row", None, None, None),
        P("col", "row"),
        P("col", "row", None),
        P("col", "row", None),
    )
    return jax.shard_map(
        local,
        mesh=mesh,
        in_specs=placed,
        out_specs=(P(("row", "col"), None), P(("row", "col"), None)),
        check_vma=False,
    )
```

```python
import jax
import jax.numpy as jnp
from jax import lax
from jax.experimental import pallas as pl
from jax.experimental.pallas import tpu as pltpu
from jax.sharding import PartitionSpec as P

ridge_weight = 0.5
LANES = 128
FLIP = 1 << 30
FIRST = (5, 5, 5)
VMEM_LIMIT = 16 << 20
F32 = jnp.float32
BF16 = jnp.bfloat16


def vmem():
    return pl.BlockSpec(memory_space=pltpu.VMEM)


def stay(x):
    return pltpu.with_memory_space_constraint(x, pltpu.HBM)


def call(body, name, out_shapes, args, in_specs=None, scratch=(), flops=0, moved=0):
    return pl.pallas_call(
        body,
        name=name,
        out_shape=[pltpu.VMEM(s, d) for s, d in out_shapes],
        in_specs=in_specs or [vmem()] * len(args),
        out_specs=[vmem()] * len(out_shapes),
        scratch_shapes=list(scratch),
        compiler_params=pltpu.CompilerParams(vmem_limit_bytes=VMEM_LIMIT),
        cost_estimate=pl.CostEstimate(flops=flops, bytes_accessed=moved, transcendentals=0),
    )(*args)


def split3(x):
    high = x.astype(BF16).astype(F32)
    rest = x - high
    middle = rest.astype(BF16).astype(F32)
    return jnp.concatenate([high, middle, rest - middle], axis=0).astype(BF16)


def lane_sum(row):
    return jnp.sum(row, axis=1, keepdims=True)


def row_sum(x):
    return jnp.sum(x, axis=0, keepdims=True)


def pieces_of(x):
    return [x[:, h : h + LANES] for h in range(0, x.shape[1], LANES)]


def fold(row):
    return sum(pieces_of(row)[1:], pieces_of(row)[0])


def put(ref, first, x):
    for piece in pieces_of(x):
        ref[pl.ds(first, piece.shape[0]), 0, :] = piece
        first += piece.shape[0]


def take(x, rows, size):
    return jnp.concatenate([x[h * rows : (h + 1) * rows] for h in range(size // LANES)], axis=1)


def block_product(spread, gather, vector, tiles, slots):
    terms = split3(vector)
    size = vector.shape[1]
    parts = []
    for k in range(0, slots, 2):
        table = spread[:, k * LANES : (k + 2) * LANES]
        wide = lax.dot_general(terms, table, (((0,), (0,)), ((), ())), preferred_element_type=F32)
        for m in range(2):
            here = wide[:, m * LANES : (m + 1) * LANES]
            row = []
            for h in range(0, size, LANES):
                product = tiles[k + m, :, h : h + LANES] * here
                row.append(jnp.sum(product.reshape(size // 8, 8, LANES), axis=0))
            parts.append(jnp.concatenate(row, axis=1))
    parts = jnp.concatenate(parts, axis=0)
    count = parts.shape[0]
    terms = split3(parts)
    total = jnp.dot(gather[...], terms[:count], preferred_element_type=F32)
    total += jnp.dot(gather[...], terms[count : 2 * count], preferred_element_type=F32)
    return total + jnp.dot(gather[...], terms[2 * count :], preferred_element_type=F32)


def flip_body(tiles, out):
    for k in range(out.shape[0]):
        out[k] = tiles[0, 0, k].T


def start_body(group, cols, slots, first, *refs):
    sources, (sent, spread_rows, spread_cols, gather_rows, gather_cols, own), held, sem = refs[:5], refs[5:11], refs[11:16], refs[16]
    copies = [pltpu.make_async_copy(a, b, sem.at[i]) for i, (a, b) in enumerate(zip(sources, held))]
    for copy in copies:
        copy.start()

    def place(index):
        return jnp.where(index >= first, index - first, index - first + group)

    mine = lax.broadcasted_iota(jnp.int32, own.shape, 0) == place(lax.axis_index("col"))
    own[...] = jnp.where(mine, 1.0, 0.0)
    for copy in copies:
        copy.wait()
    side, weights, count, rows_of, cols_of = held
    both = jnp.concatenate([side[...], weights[...]], axis=0)
    sent[...] = jnp.broadcast_to(both[None], sent.shape)

    def tables(spread, gather, extent, index):
        term = lax.broadcasted_iota(jnp.int32, (extent, LANES), 0)
        slot = lax.broadcasted_iota(jnp.int32, gather.shape, 1) // 8
        at = lax.broadcasted_iota(jnp.int32, gather.shape, 0)
        target = jnp.full(gather.shape, -1, jnp.int32)
        for k in range(slots):
            source = jnp.where(k < count[0, 0], index[k], -1)
            one = jnp.where(term == source, 1.0, 0.0)
            spread[:, pl.ds(k * LANES, LANES)] = jnp.concatenate([one] * 3, axis=0).astype(BF16)
            target = jnp.where(slot == k, index[k], target)
        gather[...] = jnp.where(at == target, 1.0, 0.0).astype(BF16)

    tables(spread_rows, gather_rows, group, [place(rows_of[0, 0, k]) for k in range(slots)])
    tables(spread_cols, gather_cols, cols, [cols_of[0, 0, k] for k in range(slots)])


def first_body(slots, cols, gathered, tiles, spread, gather, out):
    residual, weights = gathered[:, 0, :], gathered[:, 1, :]
    z = weights * residual
    size = z.shape[1]
    put(out, 0, block_product(spread, gather, z, tiles.at[0, 0], slots))
    count = cols * (size // LANES)
    put(out, count, fold(row_sum(residual * z)))
    put(out, count + 1, fold(row_sum(z * z)))


def gather4(refs):
    a, b, c, d = [r[:, 0, :] for r in refs]
    return (a + b) + (c + d)


def second_body(slots, peers, p0, p1, p2, p3, scaling, flipped, spread, gather, total, out):
    summed = gather4((p0, p1, p2, p3))
    total[...] = summed
    cols, size = scaling.shape
    lifted = take(summed, cols, size)
    weighted = scaling[...] * lifted
    inner = fold(row_sum(weighted * lifted))
    rows = block_product(spread, gather, weighted, flipped, slots)
    length = out.shape[0] // peers
    for j in range(peers):
        put(out, j * length, rows)
        put(out, (j + 1) * length - 1, inner)


def third_body(slots, cols, arrived, gathered, total, tiles, spread, gather, out, residual_out, alpha_out):
    residual, weights = gathered[:, 0, :], gathered[:, 1, :]
    z = weights * residual
    group, size = residual.shape
    length = group * (size // LANES) + 1
    peers = arrived.shape[0] // length
    summed = arrived[pl.ds(0, length), 0, :]
    for j in range(1, peers):
        summed += arrived[pl.ds(j * length, length), 0, :]
    image = take(summed, group, size) + ridge_weight * z
    count = cols * (size // LANES)
    gamma = lane_sum(total[pl.ds(count, 1), :])
    curve = lane_sum(summed[length - 1 : length] + ridge_weight * total[pl.ds(count + 1, 1), :])
    alpha = gamma / curve
    alpha_out[...] = jnp.broadcast_to(alpha, alpha_out.shape)
    later = residual - alpha * image
    residual_out[...] = later
    z1 = weights * later
    put(out, count, fold(row_sum(later * z1)))
    put(out, count + 1, fold(row_sum(z1 * z1)))
    put(out, count + 2, fold(row_sum(z1 * z)))
    put(out, 0, block_product(spread, gather, z1, tiles.at[0, 0], slots))


def fourth_body(slots, by, p0, p1, p2, p3, total, gathered, residual, scaling, flipped, spread, gather, out, direction_out, scalars):
    summed = gather4((p0, p1, p2, p3))
    cols, size = scaling.shape
    count = cols * (size // LANES)
    gamma = lane_sum(total[pl.ds(count, 1), :])
    norm = lane_sum(total[pl.ds(count + 1, 1), :])
    later = lane_sum(summed[count : count + 1])
    beta = later / gamma
    square = lane_sum(summed[count + 1 : count + 2]) + beta * (2.0 * lane_sum(summed[count + 2 : count + 3]) + beta * norm)
    lifted = take(summed, cols, size) + beta * take(total[...], cols, size)
    weighted = scaling[...] * lifted
    inner = fold(row_sum(weighted * lifted))
    rows = block_product(spread, gather, weighted, flipped, slots)
    peers = out.shape[0]
    for h, piece in enumerate(pieces_of(rows)):
        out[:, h, :] = turned(piece, by)
    out[:, size // LANES, :] = jnp.broadcast_to(inner, (peers, LANES))
    weights = gathered[:, 1, :]
    direction_out[...] = weights * residual[...] + beta * (weights * gathered[:, 0, :])
    scalars[pl.ds(0, 1), :] = jnp.broadcast_to(later, (1, LANES))
    scalars[pl.ds(1, 1), :] = jnp.broadcast_to(square, (1, LANES))


def last_body(arrived, gathered, residual, direction, alpha, scalars, own, solution, residual_out):
    size = solution.shape[1]
    mask = own[:, :1]
    summed = jnp.sum(arrived[...], axis=0)
    image = take(summed, 1, size)
    curve = lane_sum(summed[size // LANES : size // LANES + 1]) + ridge_weight * scalars[1:2, :1]
    step = scalars[0:1, :1] / curve
    first = row_sum(mask * (gathered[:, 0, :] * gathered[:, 1, :]))
    second = row_sum(mask * direction[...])
    before = row_sum(mask * residual[...])
    solution[...] = alpha[:1, :1] * first + step * second
    residual_out[...] = before - step * (image + ridge_weight * second)


def turned(x, by):
    by %= x.shape[0]
    return jnp.concatenate([x[by:], x[:by]], axis=0) if by else x


def exchange(value, size, first):
    order = [(p + first) % size for p in range(size)]
    return lax.all_to_all(value, "col", 0, 0, tiled=True, axis_index_groups=[order])


def share(value, axis, size):
    moved = [value]
    for s in range(1, size):
        moved.append(lax.ppermute(value, axis, [(i, i ^ s) for i in range(size)]))
    return moved


def local(right_side, precond, scaling, blocks, block_count, block_rows, block_cols):
    peers = lax.axis_size("col")
    groups = lax.axis_size("row")
    slots, size = blocks.shape[2], blocks.shape[3]
    own_rows = right_side.shape[0]
    assert own_rows == 1 and groups == 4
    group = own_rows * peers
    cols = scaling.shape[0]
    pieces = size // LANES
    long = slots * size
    starts = [peers * f // 8 for f in FIRST]
    work = dict(flops=8 * long * size, moved=0)

    sent, spread_rows, spread_cols, gather_rows, gather_cols, own = call(
        lambda *refs: start_body(group, cols, slots, starts[0], *refs),
        "start",
        [
            ((peers, 2, size), F32),
            ((3 * group, slots * LANES), BF16),
            ((3 * cols, slots * LANES), BF16),
            ((group, slots * 8), BF16),
            ((cols, slots * 8), BF16),
            ((group, LANES), F32),
        ],
        (stay(right_side), stay(precond), block_count, stay(block_rows), stay(block_cols)),
        in_specs=[pl.BlockSpec(memory_space=pl.ANY)] * 5,
        scratch=[
            pltpu.VMEM(right_side.shape, F32),
            pltpu.VMEM(precond.shape, F32),
            pltpu.SMEM(block_count.shape, jnp.int32),
            pltpu.SMEM(block_rows.shape, jnp.int32),
            pltpu.SMEM(block_cols.shape, jnp.int32),
            pltpu.SemaphoreType.DMA((5,)),
        ],
        flops=1 << 34,
        moved=100 << 20,
    )
    gathered = exchange(sent, peers, starts[0])
    (mine,) = call(
        lambda *refs: first_body(slots, cols, *refs),
        "first",
        [((cols * pieces + 2, 1, LANES), F32)],
        (gathered, blocks, spread_rows, gather_cols),
        **work,
    )
    (flipped,) = call(flip_body, "flip", [((slots, size, size), F32)], (blocks,), flops=FLIP)
    length = group * pieces + 1
    total, sent = call(
        lambda *refs: second_body(slots, peers, *refs),
        "second",
        [((cols * pieces + 2, LANES), F32), ((peers * length, 1, LANES), F32)],
        (*share(mine, "row", groups), scaling, flipped, spread_cols, gather_rows),
        **work,
    )
    arrived = exchange(sent, peers, starts[1])
    mine, residual, alpha = call(
        lambda *refs: third_body(slots, cols, *refs),
        "third",
        [((cols * pieces + 3, 1, LANES), F32), ((group, size), F32), ((1, LANES), F32)],
        (arrived, gathered, total, blocks, spread_rows, gather_cols),
        **work,
    )
    sent, direction, scalars = call(
        lambda *refs: fourth_body(slots, starts[2] - starts[0], *refs),
        "fourth",
        [((peers, pieces + 1, LANES), F32), ((group, size), F32), ((2, LANES), F32)],
        (*share(mine, "row", groups), total, gathered, residual, scaling, flipped, spread_cols, gather_rows),
        **work,
    )
    arrived = exchange(sent, peers, starts[2])
    return pl.pallas_call(
        last_body,
        name="last",
        out_shape=[jax.ShapeDtypeStruct(right_side.shape, F32)] * 2,
        in_specs=[vmem()] * 7,
        out_specs=[vmem()] * 2,
        compiler_params=pltpu.CompilerParams(vmem_limit_bytes=VMEM_LIMIT),
    )(arrived, gathered, residual, direction, alpha, scalars, own)


def solution(mesh):
    placed = (
        P(("row", "col"), None),
        P(("row", "col"), None),
        P("col", None),
        P("col", "row", None, None, None),
        P("col", "row"),
        P("col", "row", None),
        P("col", "row", None),
    )
    return jax.shard_map(
        local,
        mesh=mesh,
        in_specs=placed,
        out_specs=(P(("row", "col"), None), P(("row", "col"), None)),
        check_vma=False,
    )
```

```python
import jax
import jax.numpy as jnp
from jax import lax
from jax.experimental import pallas as pl
from jax.experimental.pallas import tpu as pltpu
from jax.sharding import PartitionSpec as P

ridge_weight = 0.5
LANES = 128
FLIP = 1 << 30
FIRST = (5, 5, 5)
VMEM_LIMIT = 16 << 20
F32 = jnp.float32
BF16 = jnp.bfloat16


def vmem():
    return pl.BlockSpec(memory_space=pltpu.VMEM)


def stay(x):
    return pltpu.with_memory_space_constraint(x, pltpu.HBM)


def call(body, name, out_shapes, args, in_specs=None, scratch=(), flops=0, moved=0):
    return pl.pallas_call(
        body,
        name=name,
        out_shape=[pltpu.VMEM(s, d) for s, d in out_shapes],
        in_specs=[vmem()] * len(args) if in_specs is None else in_specs,
        out_specs=[vmem()] * len(out_shapes),
        scratch_shapes=list(scratch),
        compiler_params=pltpu.CompilerParams(vmem_limit_bytes=VMEM_LIMIT),
        cost_estimate=pl.CostEstimate(flops=flops, bytes_accessed=moved, transcendentals=0),
    )(*args)


def split3(x):
    high = x.astype(BF16).astype(F32)
    rest = x - high
    middle = rest.astype(BF16).astype(F32)
    return jnp.concatenate([high, middle, rest - middle], axis=0).astype(BF16)


def lane_sum(row):
    return jnp.sum(row, axis=1, keepdims=True)


def row_sum(x):
    return jnp.sum(x, axis=0, keepdims=True)


def pieces_of(x):
    return [x[:, h : h + LANES] for h in range(0, x.shape[1], LANES)]


def fold(row):
    return sum(pieces_of(row)[1:], pieces_of(row)[0])


def put(ref, first, x):
    for piece in pieces_of(x):
        ref[pl.ds(first, piece.shape[0]), 0, :] = piece
        first += piece.shape[0]


def take(x, rows, size):
    return jnp.concatenate([x[h * rows : (h + 1) * rows] for h in range(size // LANES)], axis=1)


def block_product(spread, gather, vector, tiles, slots):
    terms = split3(vector)
    size = vector.shape[1]
    parts = []
    for k in range(0, slots, 2):
        table = spread[:, k * LANES : (k + 2) * LANES]
        wide = lax.dot_general(terms, table, (((0,), (0,)), ((), ())), preferred_element_type=F32)
        for m in range(2):
            here = wide[:, m * LANES : (m + 1) * LANES]
            row = []
            for h in range(0, size, LANES):
                product = tiles[k + m, :, h : h + LANES] * here
                row.append(jnp.sum(product.reshape(size // 8, 8, LANES), axis=0))
            parts.append(jnp.concatenate(row, axis=1))
    parts = jnp.concatenate(parts, axis=0)
    count = parts.shape[0]
    terms = split3(parts)
    total = jnp.dot(gather[...], terms[:count], preferred_element_type=F32)
    total += jnp.dot(gather[...], terms[count : 2 * count], preferred_element_type=F32)
    return total + jnp.dot(gather[...], terms[2 * count :], preferred_element_type=F32)


def flip_body(tiles, out):
    for k in range(out.shape[0]):
        out[k] = tiles[0, 0, k].T


def own_body(group, first, own):
    mine = lax.broadcasted_iota(jnp.int32, own.shape, 0) == turn(lax.axis_index("col"), group, first)
    own[...] = jnp.where(mine, 1.0, 0.0)


def turn(index, group, first):
    return jnp.where(index >= first, index - first, index - first + group)


def start_body(group, cols, slots, first, side, weights, count, rows_of, cols_of, own, sent, spread_rows, spread_cols, gather_rows, gather_cols):
    both = jnp.concatenate([side[...], weights[...]], axis=0)
    sent[...] = jnp.broadcast_to(both[None], sent.shape)

    def tables(spread, gather, extent, indices):
        term = lax.broadcasted_iota(jnp.int32, (extent, LANES), 0)
        slot = lax.broadcasted_iota(jnp.int32, gather.shape, 1) // 8
        at = lax.broadcasted_iota(jnp.int32, gather.shape, 0)
        target = jnp.full(gather.shape, -1, jnp.int32)
        for k in range(slots):
            index = indices[:, k : k + 1]
            source = jnp.where(k < count[0, 0], index, -1)
            one = jnp.where(term == source, 1.0, 0.0)
            spread[:, pl.ds(k * LANES, LANES)] = jnp.concatenate([one] * 3, axis=0).astype(BF16)
            target = jnp.where(slot == k, index, target)
        gather[...] = jnp.where(at == target, 1.0, 0.0).astype(BF16)

    tables(spread_rows, gather_rows, group, turn(rows_of[0], group, first))
    tables(spread_cols, gather_cols, cols, cols_of[0])


def first_body(slots, cols, gathered, tiles, spread, gather, out):
    residual, weights = gathered[:, 0, :], gathered[:, 1, :]
    z = weights * residual
    size = z.shape[1]
    put(out, 0, block_product(spread, gather, z, tiles.at[0, 0], slots))
    count = cols * (size // LANES)
    put(out, count, fold(row_sum(residual * z)))
    put(out, count + 1, fold(row_sum(z * z)))


def gather4(refs):
    a, b, c, d = [r[:, 0, :] for r in refs]
    return (a + b) + (c + d)


def second_body(slots, peers, p0, p1, p2, p3, scaling, flipped, spread, gather, total, out):
    summed = gather4((p0, p1, p2, p3))
    total[...] = summed
    cols, size = scaling.shape
    lifted = take(summed, cols, size)
    weighted = scaling[...] * lifted
    inner = fold(row_sum(weighted * lifted))
    rows = block_product(spread, gather, weighted, flipped, slots)
    length = out.shape[0] // peers
    for j in range(peers):
        put(out, j * length, rows)
        put(out, (j + 1) * length - 1, inner)


def third_body(slots, cols, arrived, gathered, total, tiles, spread, gather, out, residual_out, alpha_out):
    residual, weights = gathered[:, 0, :], gathered[:, 1, :]
    z = weights * residual
    group, size = residual.shape
    length = group * (size // LANES) + 1
    peers = arrived.shape[0] // length
    summed = arrived[pl.ds(0, length), 0, :]
    for j in range(1, peers):
        summed += arrived[pl.ds(j * length, length), 0, :]
    image = take(summed, group, size) + ridge_weight * z
    count = cols * (size // LANES)
    gamma = lane_sum(total[pl.ds(count, 1), :])
    curve = lane_sum(summed[length - 1 : length] + ridge_weight * total[pl.ds(count + 1, 1), :])
    alpha = gamma / curve
    alpha_out[...] = jnp.broadcast_to(alpha, alpha_out.shape)
    later = residual - alpha * image
    residual_out[...] = later
    z1 = weights * later
    put(out, count, fold(row_sum(later * z1)))
    put(out, count + 1, fold(row_sum(z1 * z1)))
    put(out, count + 2, fold(row_sum(z1 * z)))
    put(out, 0, block_product(spread, gather, z1, tiles.at[0, 0], slots))


def fourth_body(slots, by, p0, p1, p2, p3, total, gathered, residual, scaling, flipped, spread, gather, out, direction_out, scalars):
    summed = gather4((p0, p1, p2, p3))
    cols, size = scaling.shape
    count = cols * (size // LANES)
    gamma = lane_sum(total[pl.ds(count, 1), :])
    norm = lane_sum(total[pl.ds(count + 1, 1), :])
    later = lane_sum(summed[count : count + 1])
    beta = later / gamma
    square = lane_sum(summed[count + 1 : count + 2]) + beta * (2.0 * lane_sum(summed[count + 2 : count + 3]) + beta * norm)
    lifted = take(summed, cols, size) + beta * take(total[...], cols, size)
    weighted = scaling[...] * lifted
    inner = fold(row_sum(weighted * lifted))
    rows = block_product(spread, gather, weighted, flipped, slots)
    peers = out.shape[0]
    for h, piece in enumerate(pieces_of(rows)):
        out[:, h, :] = turned(piece, by)
    out[:, size // LANES, :] = jnp.broadcast_to(inner, (peers, LANES))
    weights = gathered[:, 1, :]
    direction_out[...] = weights * residual[...] + beta * (weights * gathered[:, 0, :])
    scalars[pl.ds(0, 1), :] = jnp.broadcast_to(later, (1, LANES))
    scalars[pl.ds(1, 1), :] = jnp.broadcast_to(square, (1, LANES))


def last_body(arrived, gathered, residual, direction, alpha, scalars, own, solution, residual_out):
    size = solution.shape[1]
    mask = own[:, :1]
    summed = jnp.sum(arrived[...], axis=0)
    image = take(summed, 1, size)
    curve = lane_sum(summed[size // LANES : size // LANES + 1]) + ridge_weight * scalars[1:2, :1]
    step = scalars[0:1, :1] / curve
    first = row_sum(mask * (gathered[:, 0, :] * gathered[:, 1, :]))
    second = row_sum(mask * direction[...])
    before = row_sum(mask * residual[...])
    solution[...] = alpha[:1, :1] * first + step * second
    residual_out[...] = before - step * (image + ridge_weight * second)


def turned(x, by):
    by %= x.shape[0]
    return jnp.concatenate([x[by:], x[:by]], axis=0) if by else x


def exchange(value, size, first):
    order = [(p + first) % size for p in range(size)]
    return lax.all_to_all(value, "col", 0, 0, tiled=True, axis_index_groups=[order])


def share(value, axis, size):
    moved = [value]
    for s in range(1, size):
        moved.append(lax.ppermute(value, axis, [(i, i ^ s) for i in range(size)]))
    return moved


def local(right_side, precond, scaling, blocks, block_count, block_rows, block_cols):
    peers = lax.axis_size("col")
    groups = lax.axis_size("row")
    slots, size = blocks.shape[2], blocks.shape[3]
    own_rows = right_side.shape[0]
    assert own_rows == 1 and groups == 4
    group = own_rows * peers
    cols = scaling.shape[0]
    pieces = size // LANES
    long = slots * size
    starts = [peers * f // 8 for f in FIRST]
    work = dict(flops=8 * long * size, moved=0)

    (own,) = call(
        lambda *refs: own_body(group, starts[0], *refs),
        "own",
        [((group, LANES), F32)],
        (),
        in_specs=[],
        flops=1 << 34,
    )
    sent, spread_rows, spread_cols, gather_rows, gather_cols = call(
        lambda *refs: start_body(group, cols, slots, starts[0], *refs),
        "start",
        [
            ((peers, 2, size), F32),
            ((3 * group, slots * LANES), BF16),
            ((3 * cols, slots * LANES), BF16),
            ((group, slots * 8), BF16),
            ((cols, slots * 8), BF16),
        ],
        (right_side, precond, block_count, block_rows, block_cols, own),
        in_specs=[vmem(), vmem(), pl.BlockSpec(memory_space=pltpu.SMEM), vmem(), vmem(), vmem()],
        flops=1 << 34,
        moved=100 << 20,
    )
    gathered = exchange(sent, peers, starts[0])
    (mine,) = call(
        lambda *refs: first_body(slots, cols, *refs),
        "first",
        [((cols * pieces + 2, 1, LANES), F32)],
        (gathered, blocks, spread_rows, gather_cols),
        **work,
    )
    (flipped,) = call(flip_body, "flip", [((slots, size, size), F32)], (blocks,), flops=FLIP)
    length = group * pieces + 1
    total, sent = call(
        lambda *refs: second_body(slots, peers, *refs),
        "second",
        [((cols * pieces + 2, LANES), F32), ((peers * length, 1, LANES), F32)],
        (*share(mine, "row", groups), scaling, flipped, spread_cols, gather_rows),
        **work,
    )
    arrived = exchange(sent, peers, starts[1])
    mine, residual, alpha = call(
        lambda *refs: third_body(slots, cols, *refs),
        "third",
        [((cols * pieces + 3, 1, LANES), F32), ((group, size), F32), ((1, LANES), F32)],
        (arrived, gathered, total, blocks, spread_rows, gather_cols),
        **work,
    )
    sent, direction, scalars = call(
        lambda *refs: fourth_body(slots, starts[2] - starts[0], *refs),
        "fourth",
        [((peers, pieces + 1, LANES), F32), ((group, size), F32), ((2, LANES), F32)],
        (*share(mine, "row", groups), total, gathered, residual, scaling, flipped, spread_cols, gather_rows),
        **work,
    )
    arrived = exchange(sent, peers, starts[2])
    return pl.pallas_call(
        last_body,
        name="last",
        out_shape=[jax.ShapeDtypeStruct(right_side.shape, F32)] * 2,
        in_specs=[vmem()] * 7,
        out_specs=[vmem()] * 2,
        compiler_params=pltpu.CompilerParams(vmem_limit_bytes=VMEM_LIMIT),
    )(arrived, gathered, residual, direction, alpha, scalars, own)


def solution(mesh):
    placed = (
        P(("row", "col"), None),
        P(("row", "col"), None),
        P("col", None),
        P("col", "row", None, None, None),
        P("col", "row"),
        P("col", "row", None),
        P("col", "row", None),
    )
    return jax.shard_map(
        local,
        mesh=mesh,
        in_specs=placed,
        out_specs=(P(("row", "col"), None), P(("row", "col"), None)),
        check_vma=False,
    )
```

```python
import jax
import jax.numpy as jnp
from jax import lax
from jax.experimental import pallas as pl
from jax.experimental.pallas import tpu as pltpu
from jax.sharding import PartitionSpec as P

ridge_weight = 0.5
LANES = 128
FLIP = 1 << 30
FIRST = (5, 5, 5)
SHARE = 2
VMEM_LIMIT = 16 << 20
F32 = jnp.float32
BF16 = jnp.bfloat16


def vmem():
    return pl.BlockSpec(memory_space=pltpu.VMEM)


def stay(x):
    return pltpu.with_memory_space_constraint(x, pltpu.HBM)


def call(body, name, out_shapes, args, in_specs=None, scratch=(), flops=0, moved=0):
    return pl.pallas_call(
        body,
        name=name,
        out_shape=[pltpu.VMEM(s, d) for s, d in out_shapes],
        in_specs=[vmem()] * len(args) if in_specs is None else in_specs,
        out_specs=[vmem()] * len(out_shapes),
        scratch_shapes=list(scratch),
        compiler_params=pltpu.CompilerParams(vmem_limit_bytes=VMEM_LIMIT),
        cost_estimate=pl.CostEstimate(flops=flops, bytes_accessed=moved, transcendentals=0),
    )(*args)


def split3(x):
    high = x.astype(BF16).astype(F32)
    rest = x - high
    middle = rest.astype(BF16).astype(F32)
    return jnp.concatenate([high, middle, rest - middle], axis=0).astype(BF16)


def split2(x):
    high = x.astype(BF16).astype(F32)
    return jnp.concatenate([high, x - high], axis=0).astype(BF16)


def lane_sum(row):
    return jnp.sum(row, axis=1, keepdims=True)


def row_sum(x):
    return jnp.sum(x, axis=0, keepdims=True)


def pieces_of(x):
    return [x[:, h : h + LANES] for h in range(0, x.shape[1], LANES)]


def fold(row):
    return sum(pieces_of(row)[1:], pieces_of(row)[0])


def put(ref, first, x):
    for piece in pieces_of(x):
        ref[pl.ds(first, piece.shape[0]), 0, :] = piece
        first += piece.shape[0]


def take(x, rows, size):
    return jnp.concatenate([x[h * rows : (h + 1) * rows] for h in range(size // LANES)], axis=1)


def block_product(spread, gather, vector, tiles, slots, table=None, high=None, low=None):
    terms = split3(vector)
    size = vector.shape[1]
    others = 0 if high is None else high.shape[0] // size
    if others:
        placed = jnp.dot(table[...], split2(vector), preferred_element_type=F32).astype(BF16)
        step = placed.shape[0] // others
        matrix = jnp.zeros((step, size), F32)
    turns = slots // 2
    parts = []
    for n in range(turns):
        spread_pair = spread[:, 2 * n * LANES : (2 * n + 2) * LANES]
        wide = lax.dot_general(terms, spread_pair, (((0,), (0,)), ((), ())), preferred_element_type=F32)
        for k in range(others * n // turns, others * (n + 1) // turns):
            left = placed[k * step : (k + 1) * step]
            here = slice(k * size, (k + 1) * size)
            matrix += jnp.dot(left, high[here, :], preferred_element_type=F32)
            matrix += jnp.dot(left, low[here, :], preferred_element_type=F32)
        for m in range(2):
            here = wide[:, m * LANES : (m + 1) * LANES]
            row = []
            for h in range(0, size, LANES):
                product = tiles[2 * n + m, :, h : h + LANES] * here
                row.append(jnp.sum(product.reshape(size // 8, 8, LANES), axis=0))
            parts.append(jnp.concatenate(row, axis=1))
    parts = jnp.concatenate(parts, axis=0)
    count = parts.shape[0]
    terms = split3(parts)
    gather = gather[:, :count]
    total = jnp.dot(gather, terms[:count], preferred_element_type=F32)
    total += jnp.dot(gather, terms[count : 2 * count], preferred_element_type=F32)
    total += jnp.dot(gather, terms[2 * count :], preferred_element_type=F32)
    if others:
        total += matrix[: step // 2] + matrix[step // 2 :]
    return total


def store_split(high, low, here, tile):
    upper = tile.astype(BF16)
    high[here, :] = upper
    low[here, :] = (tile - upper.astype(F32)).astype(BF16)


def flip_body(plain, group, cols, first, tiles, count, rows_of, cols_of, spread_cols, gather_rows, to_cols, to_rows, flipped, high, low, high_t, low_t):
    slots, size = tiles.shape[2], tiles.shape[3]
    for k in range(plain):
        flipped[k] = tiles[0, 0, k].T
    for k in range(plain, slots):
        here = pl.ds((k - plain) * size, size)
        store_split(high, low, here, tiles[0, 0, k])
        store_split(high_t, low_t, here, tiles[0, 0, k].T)
    rows, columns = turn(rows_of[0], group, first), cols_of[0]
    spread_table(spread_cols, columns, count, plain)
    gather_table(gather_rows, rows)
    for out, targets, sources, target, source in (
        (to_cols, cols, group, columns, rows),
        (to_rows, group, cols, rows, columns),
    ):
        r = lax.broadcasted_iota(jnp.int32, (2 * targets, 2 * sources), 0)
        q = lax.broadcasted_iota(jnp.int32, (2 * targets, 2 * sources), 1)
        for k in range(plain, slots):
            t = jnp.where(k < count[0, 0], target[:, k : k + 1], -1 - targets)
            s = source[:, k : k + 1]
            hit = ((r == t) & (q == s)) | ((r == targets + t) & (q == sources + s))
            out[pl.ds((k - plain) * 2 * targets, 2 * targets), :] = jnp.where(hit, 1.0, 0.0).astype(BF16)


def own_body(group, first, own):
    mine = lax.broadcasted_iota(jnp.int32, own.shape, 0) == turn(lax.axis_index("col"), group, first)
    own[...] = jnp.where(mine, 1.0, 0.0)


def turn(index, group, first):
    return jnp.where(index >= first, index - first, index - first + group)


def spread_table(out, indices, count, slots):
    term = lax.broadcasted_iota(jnp.int32, (out.shape[0] // 3, LANES), 0)
    for k in range(slots):
        source = jnp.where(k < count[0, 0], indices[:, k : k + 1], -1)
        one = jnp.where(term == source, 1.0, 0.0)
        out[:, pl.ds(k * LANES, LANES)] = jnp.concatenate([one] * 3, axis=0).astype(BF16)


def gather_table(out, indices):
    slot = lax.broadcasted_iota(jnp.int32, out.shape, 1) // 8
    at = lax.broadcasted_iota(jnp.int32, out.shape, 0)
    target = jnp.full(out.shape, -1, jnp.int32)
    for k in range(out.shape[1] // 8):
        target = jnp.where(slot == k, indices[:, k : k + 1], target)
    out[...] = jnp.where(at == target, 1.0, 0.0).astype(BF16)


def start_body(group, slots, first, side, weights, count, rows_of, cols_of, own, sent, spread_rows, gather_cols):
    both = jnp.concatenate([side[...], weights[...]], axis=0)
    sent[...] = jnp.broadcast_to(both[None], sent.shape)
    spread_table(spread_rows, turn(rows_of[0], group, first), count, slots)
    gather_table(gather_cols, cols_of[0])


def first_body(slots, cols, gathered, tiles, spread, gather, out):
    residual, weights = gathered[:, 0, :], gathered[:, 1, :]
    z = weights * residual
    size = z.shape[1]
    put(out, 0, block_product(spread, gather, z, tiles.at[0, 0], slots))
    count = cols * (size // LANES)
    put(out, count, fold(row_sum(residual * z)))
    put(out, count + 1, fold(row_sum(z * z)))


def gather4(refs):
    a, b, c, d = [r[:, 0, :] for r in refs]
    return (a + b) + (c + d)


def second_body(slots, peers, p0, p1, p2, p3, scaling, flipped, spread, gather, table, high, low, total, out):
    summed = gather4((p0, p1, p2, p3))
    total[...] = summed
    cols, size = scaling.shape
    lifted = take(summed, cols, size)
    weighted = scaling[...] * lifted
    inner = fold(row_sum(weighted * lifted))
    rows = block_product(spread, gather, weighted, flipped, slots, table, high, low)
    length = out.shape[0] // peers
    for j in range(peers):
        put(out, j * length, rows)
        put(out, (j + 1) * length - 1, inner)


def third_body(slots, cols, arrived, gathered, total, tiles, spread, gather, table, high, low, out, residual_out, alpha_out):
    residual, weights = gathered[:, 0, :], gathered[:, 1, :]
    z = weights * residual
    group, size = residual.shape
    length = group * (size // LANES) + 1
    peers = arrived.shape[0] // length
    summed = arrived[pl.ds(0, length), 0, :]
    for j in range(1, peers):
        summed += arrived[pl.ds(j * length, length), 0, :]
    image = take(summed, group, size) + ridge_weight * z
    count = cols * (size // LANES)
    gamma = lane_sum(total[pl.ds(count, 1), :])
    curve = lane_sum(summed[length - 1 : length] + ridge_weight * total[pl.ds(count + 1, 1), :])
    alpha = gamma / curve
    alpha_out[...] = jnp.broadcast_to(alpha, alpha_out.shape)
    later = residual - alpha * image
    residual_out[...] = later
    z1 = weights * later
    put(out, count, fold(row_sum(later * z1)))
    put(out, count + 1, fold(row_sum(z1 * z1)))
    put(out, count + 2, fold(row_sum(z1 * z)))
    put(out, 0, block_product(spread, gather, z1, tiles.at[0, 0], slots, table, high, low))


def fourth_body(slots, by, p0, p1, p2, p3, total, gathered, residual, scaling, flipped, spread, gather, table, high, low, out, direction_out, scalars):
    summed = gather4((p0, p1, p2, p3))
    cols, size = scaling.shape
    count = cols * (size // LANES)
    gamma = lane_sum(total[pl.ds(count, 1), :])
    norm = lane_sum(total[pl.ds(count + 1, 1), :])
    later = lane_sum(summed[count : count + 1])
    beta = later / gamma
    square = lane_sum(summed[count + 1 : count + 2]) + beta * (2.0 * lane_sum(summed[count + 2 : count + 3]) + beta * norm)
    lifted = take(summed, cols, size) + beta * take(total[...], cols, size)
    weighted = scaling[...] * lifted
    inner = fold(row_sum(weighted * lifted))
    rows = block_product(spread, gather, weighted, flipped, slots, table, high, low)
    peers = out.shape[0]
    for h, piece in enumerate(pieces_of(rows)):
        out[:, h, :] = turned(piece, by)
    out[:, size // LANES, :] = jnp.broadcast_to(inner, (peers, LANES))
    weights = gathered[:, 1, :]
    direction_out[...] = weights * residual[...] + beta * (weights * gathered[:, 0, :])
    scalars[pl.ds(0, 1), :] = jnp.broadcast_to(later, (1, LANES))
    scalars[pl.ds(1, 1), :] = jnp.broadcast_to(square, (1, LANES))


def last_body(arrived, gathered, residual, direction, alpha, scalars, own, solution, residual_out):
    size = solution.shape[1]
    mask = own[:, :1]
    summed = jnp.sum(arrived[...], axis=0)
    image = take(summed, 1, size)
    curve = lane_sum(summed[size // LANES : size // LANES + 1]) + ridge_weight * scalars[1:2, :1]
    step = scalars[0:1, :1] / curve
    first = row_sum(mask * (gathered[:, 0, :] * gathered[:, 1, :]))
    second = row_sum(mask * direction[...])
    before = row_sum(mask * residual[...])
    solution[...] = alpha[:1, :1] * first + step * second
    residual_out[...] = before - step * (image + ridge_weight * second)


def turned(x, by):
    by %= x.shape[0]
    return jnp.concatenate([x[by:], x[:by]], axis=0) if by else x


def exchange(value, size, first):
    order = [(p + first) % size for p in range(size)]
    return lax.all_to_all(value, "col", 0, 0, tiled=True, axis_index_groups=[order])


def share(value, axis, size):
    moved = [value]
    for s in range(1, size):
        moved.append(lax.ppermute(value, axis, [(i, i ^ s) for i in range(size)]))
    return moved


def local(right_side, precond, scaling, blocks, block_count, block_rows, block_cols):
    peers = lax.axis_size("col")
    groups = lax.axis_size("row")
    slots, size = blocks.shape[2], blocks.shape[3]
    own_rows = right_side.shape[0]
    assert own_rows == 1 and groups == 4
    group = own_rows * peers
    cols = scaling.shape[0]
    pieces = size // LANES
    long = slots * size
    starts = [peers * f // 8 for f in FIRST]
    work = dict(flops=8 * long * size, moved=0)

    (own,) = call(
        lambda *refs: own_body(group, starts[0], *refs),
        "own",
        [((group, LANES), F32)],
        (),
        in_specs=[],
        flops=1 << 34,
    )
    sent, spread_rows, gather_cols = call(
        lambda *refs: start_body(group, slots, starts[0], *refs),
        "start",
        [((peers, 2, size), F32), ((3 * group, slots * LANES), BF16), ((cols, slots * 8), BF16)],
        (right_side, precond, block_count, block_rows, block_cols, own),
        in_specs=[vmem(), vmem(), pl.BlockSpec(memory_space=pltpu.SMEM), vmem(), vmem(), vmem()],
        flops=1 << 34,
        moved=100 << 20,
    )
    gathered = exchange(sent, peers, starts[0])
    (mine,) = call(
        lambda *refs: first_body(slots, cols, *refs),
        "first",
        [((cols * pieces + 2, 1, LANES), F32)],
        (gathered, blocks, spread_rows, gather_cols),
        **work,
    )
    plain = (slots - slots * SHARE // 16) // 2 * 2
    rest = slots - plain
    spread_cols, gather_rows, to_cols, to_rows, flipped, high, low, high_t, low_t = call(
        lambda *refs: flip_body(plain, group, cols, starts[0], *refs),
        "flip",
        [
            ((3 * cols, plain * LANES), BF16),
            ((group, plain * 8), BF16),
            ((rest * 2 * cols, 2 * group), BF16),
            ((rest * 2 * group, 2 * cols), BF16),
            ((plain, size, size), F32),
        ]
        + [((rest * size, size), BF16)] * 4,
        (blocks, block_count, block_rows, block_cols),
        in_specs=[vmem(), pl.BlockSpec(memory_space=pltpu.SMEM), vmem(), vmem()],
        flops=FLIP,
    )
    length = group * pieces + 1
    total, sent = call(
        lambda *refs: second_body(plain, peers, *refs),
        "second",
        [((cols * pieces + 2, LANES), F32), ((peers * length, 1, LANES), F32)],
        (*share(mine, "row", groups), scaling, flipped, spread_cols, gather_rows, to_rows, high_t, low_t),
        **work,
    )
    arrived = exchange(sent, peers, starts[1])
    mine, residual, alpha = call(
        lambda *refs: third_body(plain, cols, *refs),
        "third",
        [((cols * pieces + 3, 1, LANES), F32), ((group, size), F32), ((1, LANES), F32)],
        (arrived, gathered, total, blocks, spread_rows, gather_cols, to_cols, high, low),
        **work,
    )
    sent, direction, scalars = call(
        lambda *refs: fourth_body(plain, starts[2] - starts[0], *refs),
        "fourth",
        [((peers, pieces + 1, LANES), F32), ((group, size), F32), ((2, LANES), F32)],
        (*share(mine, "row", groups), total, gathered, residual, scaling, flipped, spread_cols, gather_rows, to_rows, high_t, low_t),
        **work,
    )
    arrived = exchange(sent, peers, starts[2])
    return pl.pallas_call(
        last_body,
        name="last",
        out_shape=[jax.ShapeDtypeStruct(right_side.shape, F32)] * 2,
        in_specs=[vmem()] * 7,
        out_specs=[vmem()] * 2,
        compiler_params=pltpu.CompilerParams(vmem_limit_bytes=VMEM_LIMIT),
    )(arrived, gathered, residual, direction, alpha, scalars, own)


def solution(mesh):
    placed = (
        P(("row", "col"), None),
        P(("row", "col"), None),
        P("col", None),
        P("col", "row", None, None, None),
        P("col", "row"),
        P("col", "row", None),
        P("col", "row", None),
    )
    return jax.shard_map(
        local,
        mesh=mesh,
        in_specs=placed,
        out_specs=(P(("row", "col"), None), P(("row", "col"), None)),
        check_vma=False,
    )
```

```python
import jax
import jax.numpy as jnp
from jax import lax
from jax.experimental import pallas as pl
from jax.experimental.pallas import tpu as pltpu
from jax.sharding import PartitionSpec as P

ridge_weight = 0.5
LANES = 128
FLIP = 1 << 30
FIRST = (5, 5, 5)
SHARE = 2
VMEM_LIMIT = 16 << 20
F32 = jnp.float32
BF16 = jnp.bfloat16


def vmem():
    return pl.BlockSpec(memory_space=pltpu.VMEM)


def stay(x):
    return pltpu.with_memory_space_constraint(x, pltpu.HBM)


def call(body, name, out_shapes, args, in_specs=None, scratch=(), flops=0, moved=0):
    return pl.pallas_call(
        body,
        name=name,
        out_shape=[pltpu.VMEM(s, d) for s, d in out_shapes],
        in_specs=[vmem()] * len(args) if in_specs is None else in_specs,
        out_specs=[vmem()] * len(out_shapes),
        scratch_shapes=list(scratch),
        compiler_params=pltpu.CompilerParams(vmem_limit_bytes=VMEM_LIMIT),
        cost_estimate=pl.CostEstimate(flops=flops, bytes_accessed=moved, transcendentals=0),
    )(*args)


def split3(x):
    high = x.astype(BF16).astype(F32)
    rest = x - high
    middle = rest.astype(BF16).astype(F32)
    return jnp.concatenate([high, middle, rest - middle], axis=0).astype(BF16)


def split2(x):
    high = x.astype(BF16).astype(F32)
    return jnp.concatenate([high, x - high], axis=0).astype(BF16)


def lane_sum(row):
    return jnp.sum(row, axis=1, keepdims=True)


def row_sum(x):
    return jnp.sum(x, axis=0, keepdims=True)


def pieces_of(x):
    return [x[:, h : h + LANES] for h in range(0, x.shape[1], LANES)]


def fold(row):
    return sum(pieces_of(row)[1:], pieces_of(row)[0])


def put(ref, first, x):
    for piece in pieces_of(x):
        ref[pl.ds(first, piece.shape[0]), 0, :] = piece
        first += piece.shape[0]


def take(x, rows, size):
    return jnp.concatenate([x[h * rows : (h + 1) * rows] for h in range(size // LANES)], axis=1)


def block_product(spread, gather, vector, tiles, slots, table=None, high=None, low=None):
    terms = split3(vector)
    size = vector.shape[1]
    others = 0 if high is None else high.shape[0] // size
    if others:
        placed = jnp.dot(table[...], split2(vector), preferred_element_type=F32).astype(BF16)
        step = placed.shape[0] // others
        matrix = jnp.zeros((step, size), F32)
    turns = slots // 2
    parts = []
    for n in range(turns):
        spread_pair = spread[:, 2 * n * LANES : (2 * n + 2) * LANES]
        wide = lax.dot_general(terms, spread_pair, (((0,), (0,)), ((), ())), preferred_element_type=F32)
        for k in range(others * n // turns, others * (n + 1) // turns):
            left = placed[k * step : (k + 1) * step]
            here = slice(k * size, (k + 1) * size)
            matrix += jnp.dot(left, high[here, :], preferred_element_type=F32)
            matrix += jnp.dot(left, low[here, :], preferred_element_type=F32)
        for m in range(2):
            here = wide[:, m * LANES : (m + 1) * LANES]
            row = []
            for h in range(0, size, LANES):
                product = tiles[2 * n + m, :, h : h + LANES] * here
                row.append(jnp.sum(product.reshape(size // 8, 8, LANES), axis=0))
            parts.append(jnp.concatenate(row, axis=1))
    parts = jnp.concatenate(parts, axis=0)
    count = parts.shape[0]
    terms = split3(parts)
    gather = gather[:, :count]
    total = jnp.dot(gather, terms[:count], preferred_element_type=F32)
    total += jnp.dot(gather, terms[count : 2 * count], preferred_element_type=F32)
    total += jnp.dot(gather, terms[2 * count :], preferred_element_type=F32)
    if others:
        total += matrix[: step // 2] + matrix[step // 2 :]
    return total


def store_split(high, low, here, tile):
    upper = tile.astype(BF16)
    high[here, :] = upper
    low[here, :] = (tile - upper.astype(F32)).astype(BF16)


def flip_body(plain, group, cols, first, tiles, count, rows_of, cols_of, spread_cols, gather_rows, to_cols, to_rows, flipped, high, low, high_t, low_t):
    slots, size = tiles.shape[2], tiles.shape[3]
    for k in range(plain):
        flipped[k] = tiles[0, 0, k].T
    for k in range(plain, slots):
        here = pl.ds((k - plain) * size, size)
        store_split(high, low, here, tiles[0, 0, k])
        store_split(high_t, low_t, here, tiles[0, 0, k].T)
    rows, columns = turn(rows_of[0], group, first), cols_of[0]
    spread_table(spread_cols, columns, count, plain)
    gather_table(gather_rows, rows)
    for out, targets, sources, target, source in (
        (to_cols, cols, group, columns, rows),
        (to_rows, group, cols, rows, columns),
    ):
        r = lax.broadcasted_iota(jnp.int32, (2 * targets, 2 * sources), 0)
        q = lax.broadcasted_iota(jnp.int32, (2 * targets, 2 * sources), 1)
        for k in range(plain, slots):
            t = jnp.where(k < count[0, 0], target[:, k : k + 1], -1 - targets)
            s = source[:, k : k + 1]
            hit = ((r == t) & (q == s)) | ((r == targets + t) & (q == sources + s))
            out[pl.ds((k - plain) * 2 * targets, 2 * targets), :] = jnp.where(hit, 1.0, 0.0).astype(BF16)


def own_body(group, first, own):
    mine = lax.broadcasted_iota(jnp.int32, own.shape, 0) == turn(lax.axis_index("col"), group, first)
    own[...] = jnp.where(mine, 1.0, 0.0)


def turn(index, group, first):
    return jnp.where(index >= first, index - first, index - first + group)


def spread_table(out, indices, count, slots):
    term = lax.broadcasted_iota(jnp.int32, (out.shape[0] // 3, LANES), 0)
    for k in range(slots):
        source = jnp.where(k < count[0, 0], indices[:, k : k + 1], -1)
        one = jnp.where(term == source, 1.0, 0.0)
        out[:, pl.ds(k * LANES, LANES)] = jnp.concatenate([one] * 3, axis=0).astype(BF16)


def gather_table(out, indices):
    slot = lax.broadcasted_iota(jnp.int32, out.shape, 1) // 8
    at = lax.broadcasted_iota(jnp.int32, out.shape, 0)
    target = jnp.full(out.shape, -1, jnp.int32)
    for k in range(out.shape[1] // 8):
        target = jnp.where(slot == k, indices[:, k : k + 1], target)
    out[...] = jnp.where(at == target, 1.0, 0.0).astype(BF16)


def start_body(group, slots, first, side, weights, count, rows_of, cols_of, own, sent, spread_rows, gather_cols):
    both = jnp.concatenate([side[...], weights[...]], axis=0)
    sent[...] = jnp.broadcast_to(both[None], sent.shape)
    spread_table(spread_rows, turn(rows_of[0], group, first), count, slots)
    gather_table(gather_cols, cols_of[0])


def first_body(slots, cols, gathered, tiles, spread, gather, out):
    residual, weights = gathered[:, 0, :], gathered[:, 1, :]
    z = weights * residual
    size = z.shape[1]
    put(out, 0, block_product(spread, gather, z, tiles.at[0, 0], slots))
    count = cols * (size // LANES)
    put(out, count, fold(row_sum(residual * z)))
    put(out, count + 1, fold(row_sum(z * z)))


def gather4(refs):
    a, b, c, d = [r[:, 0, :] for r in refs]
    return (a + b) + (c + d)


def second_body(slots, peers, p0, p1, p2, p3, scaling, flipped, spread, gather, table, high, low, total, out):
    summed = gather4((p0, p1, p2, p3))
    total[...] = summed
    cols, size = scaling.shape
    lifted = take(summed, cols, size)
    weighted = scaling[...] * lifted
    inner = fold(row_sum(weighted * lifted))
    rows = block_product(spread, gather, weighted, flipped, slots, table, high, low)
    length = out.shape[0] // peers
    packed = jnp.concatenate(pieces_of(rows) + [inner], axis=0)
    for j in range(peers):
        out[pl.ds(j * length, length), :] = packed


def third_body(slots, cols, arrived, gathered, total, tiles, spread, gather, table, high, low, out, residual_out, alpha_out):
    residual, weights = gathered[:, 0, :], gathered[:, 1, :]
    z = weights * residual
    group, size = residual.shape
    length = group * (size // LANES) + 1
    peers = arrived.shape[0] // length
    summed = arrived[pl.ds(0, length), :]
    for j in range(1, peers):
        summed += arrived[pl.ds(j * length, length), :]
    image = take(summed, group, size) + ridge_weight * z
    count = cols * (size // LANES)
    gamma = lane_sum(total[pl.ds(count, 1), :])
    curve = lane_sum(summed[length - 1 : length] + ridge_weight * total[pl.ds(count + 1, 1), :])
    alpha = gamma / curve
    alpha_out[...] = jnp.broadcast_to(alpha, alpha_out.shape)
    later = residual - alpha * image
    residual_out[...] = later
    z1 = weights * later
    put(out, count, fold(row_sum(later * z1)))
    put(out, count + 1, fold(row_sum(z1 * z1)))
    put(out, count + 2, fold(row_sum(z1 * z)))
    put(out, 0, block_product(spread, gather, z1, tiles.at[0, 0], slots, table, high, low))


def fourth_body(slots, by, p0, p1, p2, p3, total, gathered, residual, scaling, flipped, spread, gather, table, high, low, out, direction_out, scalars):
    summed = gather4((p0, p1, p2, p3))
    cols, size = scaling.shape
    count = cols * (size // LANES)
    gamma = lane_sum(total[pl.ds(count, 1), :])
    norm = lane_sum(total[pl.ds(count + 1, 1), :])
    later = lane_sum(summed[count : count + 1])
    beta = later / gamma
    square = lane_sum(summed[count + 1 : count + 2]) + beta * (2.0 * lane_sum(summed[count + 2 : count + 3]) + beta * norm)
    lifted = take(summed, cols, size) + beta * take(total[...], cols, size)
    weighted = scaling[...] * lifted
    inner = fold(row_sum(weighted * lifted))
    rows = block_product(spread, gather, weighted, flipped, slots, table, high, low)
    peers = out.shape[0]
    for h, piece in enumerate(pieces_of(rows)):
        out[:, h, :] = turned(piece, by)
    out[:, size // LANES, :] = jnp.broadcast_to(inner, (peers, LANES))
    weights = gathered[:, 1, :]
    direction_out[...] = weights * residual[...] + beta * (weights * gathered[:, 0, :])
    scalars[pl.ds(0, 1), :] = jnp.broadcast_to(later, (1, LANES))
    scalars[pl.ds(1, 1), :] = jnp.broadcast_to(square, (1, LANES))


def last_body(arrived, gathered, residual, direction, alpha, scalars, own, solution, residual_out):
    size = solution.shape[1]
    mask = own[:, :1]
    summed = jnp.sum(arrived[...], axis=0)
    image = take(summed, 1, size)
    curve = lane_sum(summed[size // LANES : size // LANES + 1]) + ridge_weight * scalars[1:2, :1]
    step = scalars[0:1, :1] / curve
    first = row_sum(mask * (gathered[:, 0, :] * gathered[:, 1, :]))
    second = row_sum(mask * direction[...])
    before = row_sum(mask * residual[...])
    solution[...] = alpha[:1, :1] * first + step * second
    residual_out[...] = before - step * (image + ridge_weight * second)


def turned(x, by):
    by %= x.shape[0]
    return jnp.concatenate([x[by:], x[:by]], axis=0) if by else x


def exchange(value, size, first):
    order = [(p + first) % size for p in range(size)]
    return lax.all_to_all(value, "col", 0, 0, tiled=True, axis_index_groups=[order])


def share(value, axis, size):
    moved = [value]
    for s in range(1, size):
        moved.append(lax.ppermute(value, axis, [(i, i ^ s) for i in range(size)]))
    return moved


def local(right_side, precond, scaling, blocks, block_count, block_rows, block_cols):
    peers = lax.axis_size("col")
    groups = lax.axis_size("row")
    slots, size = blocks.shape[2], blocks.shape[3]
    own_rows = right_side.shape[0]
    assert own_rows == 1 and groups == 4
    group = own_rows * peers
    cols = scaling.shape[0]
    pieces = size // LANES
    long = slots * size
    starts = [peers * f // 8 for f in FIRST]
    work = dict(flops=8 * long * size, moved=0)

    (own,) = call(
        lambda *refs: own_body(group, starts[0], *refs),
        "own",
        [((group, LANES), F32)],
        (),
        in_specs=[],
        flops=1 << 34,
    )
    sent, spread_rows, gather_cols = call(
        lambda *refs: start_body(group, slots, starts[0], *refs),
        "start",
        [((peers, 2, size), F32), ((3 * group, slots * LANES), BF16), ((cols, slots * 8), BF16)],
        (right_side, precond, block_count, block_rows, block_cols, own),
        in_specs=[vmem(), vmem(), pl.BlockSpec(memory_space=pltpu.SMEM), vmem(), vmem(), vmem()],
        flops=1 << 34,
        moved=100 << 20,
    )
    gathered = exchange(sent, peers, starts[0])
    (mine,) = call(
        lambda *refs: first_body(slots, cols, *refs),
        "first",
        [((cols * pieces + 2, 1, LANES), F32)],
        (gathered, blocks, spread_rows, gather_cols),
        **work,
    )
    plain = (slots - slots * SHARE // 16) // 2 * 2
    rest = slots - plain
    spread_cols, gather_rows, to_cols, to_rows, flipped, high, low, high_t, low_t = call(
        lambda *refs: flip_body(plain, group, cols, starts[0], *refs),
        "flip",
        [
            ((3 * cols, plain * LANES), BF16),
            ((group, plain * 8), BF16),
            ((rest * 2 * cols, 2 * group), BF16),
            ((rest * 2 * group, 2 * cols), BF16),
            ((plain, size, size), F32),
        ]
        + [((rest * size, size), BF16)] * 4,
        (blocks, block_count, block_rows, block_cols),
        in_specs=[vmem(), pl.BlockSpec(memory_space=pltpu.SMEM), vmem(), vmem()],
        flops=FLIP,
    )
    length = group * pieces + 1
    total, sent = call(
        lambda *refs: second_body(plain, peers, *refs),
        "second",
        [((cols * pieces + 2, LANES), F32), ((peers * length, LANES), F32)],
        (*share(mine, "row", groups), scaling, flipped, spread_cols, gather_rows, to_rows, high_t, low_t),
        **work,
    )
    arrived = exchange(sent.reshape(-1, 1, LANES), peers, starts[1])
    mine, residual, alpha = call(
        lambda *refs: third_body(plain, cols, *refs),
        "third",
        [((cols * pieces + 3, 1, LANES), F32), ((group, size), F32), ((1, LANES), F32)],
        (arrived.reshape(-1, LANES), gathered, total, blocks, spread_rows, gather_cols, to_cols, high, low),
        **work,
    )
    sent, direction, scalars = call(
        lambda *refs: fourth_body(plain, starts[2] - starts[0], *refs),
        "fourth",
        [((peers, pieces + 1, LANES), F32), ((group, size), F32), ((2, LANES), F32)],
        (*share(mine, "row", groups), total, gathered, residual, scaling, flipped, spread_cols, gather_rows, to_rows, high_t, low_t),
        **work,
    )
    arrived = exchange(sent, peers, starts[2])
    return pl.pallas_call(
        last_body,
        name="last",
        out_shape=[jax.ShapeDtypeStruct(right_side.shape, F32)] * 2,
        in_specs=[vmem()] * 7,
        out_specs=[vmem()] * 2,
        compiler_params=pltpu.CompilerParams(vmem_limit_bytes=VMEM_LIMIT),
    )(arrived, gathered, residual, direction, alpha, scalars, own)


def solution(mesh):
    placed = (
        P(("row", "col"), None),
        P(("row", "col"), None),
        P("col", None),
        P("col", "row", None, None, None),
        P("col", "row"),
        P("col", "row", None),
        P("col", "row", None),
    )
    return jax.shard_map(
        local,
        mesh=mesh,
        in_specs=placed,
        out_specs=(P(("row", "col"), None), P(("row", "col"), None)),
        check_vma=False,
    )
```

```python
import jax
import jax.numpy as jnp
from jax import lax
from jax.experimental import pallas as pl
from jax.experimental.pallas import tpu as pltpu
from jax.sharding import PartitionSpec as P

ridge_weight = 0.5
LANES = 128
FLIP = 1 << 30
FIRST = (5, 5, 5)
SHARE = 0
VMEM_LIMIT = 16 << 20
F32 = jnp.float32
BF16 = jnp.bfloat16


def vmem():
    return pl.BlockSpec(memory_space=pltpu.VMEM)


def stay(x):
    return pltpu.with_memory_space_constraint(x, pltpu.HBM)


def call(body, name, out_shapes, args, in_specs=None, scratch=(), flops=0, moved=0):
    return pl.pallas_call(
        body,
        name=name,
        out_shape=[pltpu.VMEM(s, d) for s, d in out_shapes],
        in_specs=[vmem()] * len(args) if in_specs is None else in_specs,
        out_specs=[vmem()] * len(out_shapes),
        scratch_shapes=list(scratch),
        compiler_params=pltpu.CompilerParams(vmem_limit_bytes=VMEM_LIMIT),
        cost_estimate=pl.CostEstimate(flops=flops, bytes_accessed=moved, transcendentals=0),
    )(*args)


def split3(x):
    high = x.astype(BF16).astype(F32)
    rest = x - high
    middle = rest.astype(BF16).astype(F32)
    return jnp.concatenate([high, middle, rest - middle], axis=0).astype(BF16)


def split2(x):
    high = x.astype(BF16).astype(F32)
    return jnp.concatenate([high, x - high], axis=0).astype(BF16)


def lane_sum(row):
    return jnp.sum(row, axis=1, keepdims=True)


def row_sum(x):
    return jnp.sum(x, axis=0, keepdims=True)


def pieces_of(x):
    return [x[:, h : h + LANES] for h in range(0, x.shape[1], LANES)]


def fold(row):
    return sum(pieces_of(row)[1:], pieces_of(row)[0])


def put(ref, first, x):
    for piece in pieces_of(x):
        ref[pl.ds(first, piece.shape[0]), 0, :] = piece
        first += piece.shape[0]


def take(x, rows, size):
    return jnp.concatenate([x[h * rows : (h + 1) * rows] for h in range(size // LANES)], axis=1)


def block_product(spread, gather, vector, tiles, slots, table=None, high=None, low=None):
    terms = split3(vector)
    size = vector.shape[1]
    others = 0 if high is None else high.shape[0] // size
    if others:
        placed = jnp.dot(table[...], split2(vector), preferred_element_type=F32).astype(BF16)
        step = placed.shape[0] // others
        matrix = jnp.zeros((step, size), F32)
    turns = slots // 2
    parts = []
    for n in range(turns):
        spread_pair = spread[:, 2 * n * LANES : (2 * n + 2) * LANES]
        wide = lax.dot_general(terms, spread_pair, (((0,), (0,)), ((), ())), preferred_element_type=F32)
        for k in range(others * n // turns, others * (n + 1) // turns):
            left = placed[k * step : (k + 1) * step]
            here = slice(k * size, (k + 1) * size)
            matrix += jnp.dot(left, high[here, :], preferred_element_type=F32)
            matrix += jnp.dot(left, low[here, :], preferred_element_type=F32)
        for m in range(2):
            here = wide[:, m * LANES : (m + 1) * LANES]
            row = []
            for h in range(0, size, LANES):
                product = tiles[2 * n + m, :, h : h + LANES] * here
                row.append(jnp.sum(product.reshape(size // 8, 8, LANES), axis=0))
            parts.append(jnp.concatenate(row, axis=1))
    parts = jnp.concatenate(parts, axis=0)
    count = parts.shape[0]
    terms = split3(parts)
    gather = gather[:, :count]
    total = jnp.dot(gather, terms[:count], preferred_element_type=F32)
    total += jnp.dot(gather, terms[count : 2 * count], preferred_element_type=F32)
    total += jnp.dot(gather, terms[2 * count :], preferred_element_type=F32)
    if others:
        total += matrix[: step // 2] + matrix[step // 2 :]
    return total


def store_split(high, low, here, tile):
    upper = tile.astype(BF16)
    high[here, :] = upper
    low[here, :] = (tile - upper.astype(F32)).astype(BF16)


def flip_body(plain, group, cols, first, tiles, count, rows_of, cols_of, spread_cols, gather_rows, flipped):
    slots, size = tiles.shape[2], tiles.shape[3]
    for k in range(plain):
        flipped[k] = tiles[0, 0, k].T
    rows, columns = turn(rows_of[0], group, first), cols_of[0]
    spread_table(spread_cols, columns, count, plain)
    gather_table(gather_rows, rows)


def own_body(group, first, own):
    mine = lax.broadcasted_iota(jnp.int32, own.shape, 0) == turn(lax.axis_index("col"), group, first)
    own[...] = jnp.where(mine, 1.0, 0.0)


def turn(index, group, first):
    return jnp.where(index >= first, index - first, index - first + group)


def spread_table(out, indices, count, slots):
    term = lax.broadcasted_iota(jnp.int32, (out.shape[0] // 3, LANES), 0)
    for k in range(slots):
        source = jnp.where(k < count[0, 0], indices[:, k : k + 1], -1)
        one = jnp.where(term == source, 1.0, 0.0)
        out[:, pl.ds(k * LANES, LANES)] = jnp.concatenate([one] * 3, axis=0).astype(BF16)


def gather_table(out, indices):
    slot = lax.broadcasted_iota(jnp.int32, out.shape, 1) // 8
    at = lax.broadcasted_iota(jnp.int32, out.shape, 0)
    target = jnp.full(out.shape, -1, jnp.int32)
    for k in range(out.shape[1] // 8):
        target = jnp.where(slot == k, indices[:, k : k + 1], target)
    out[...] = jnp.where(at == target, 1.0, 0.0).astype(BF16)


def start_body(group, slots, first, side, weights, count, rows_of, cols_of, own, sent, spread_rows, gather_cols):
    both = jnp.concatenate([side[...], weights[...]], axis=0)
    sent[...] = jnp.broadcast_to(both[None], sent.shape)
    spread_table(spread_rows, turn(rows_of[0], group, first), count, slots)
    gather_table(gather_cols, cols_of[0])


def first_body(slots, cols, gathered, tiles, spread, gather, out):
    residual, weights = gathered[:, 0, :], gathered[:, 1, :]
    z = weights * residual
    size = z.shape[1]
    put(out, 0, block_product(spread, gather, z, tiles.at[0, 0], slots))
    count = cols * (size // LANES)
    put(out, count, fold(row_sum(residual * z)))
    put(out, count + 1, fold(row_sum(z * z)))


def gather4(refs):
    a, b, c, d = [r[:, 0, :] for r in refs]
    return (a + b) + (c + d)


def second_body(slots, peers, p0, p1, p2, p3, scaling, flipped, spread, gather, total, out):
    summed = gather4((p0, p1, p2, p3))
    total[...] = summed
    cols, size = scaling.shape
    lifted = take(summed, cols, size)
    weighted = scaling[...] * lifted
    inner = fold(row_sum(weighted * lifted))
    rows = block_product(spread, gather, weighted, flipped, slots)
    length = out.shape[0] // peers
    packed = jnp.concatenate(pieces_of(rows) + [inner], axis=0)
    for j in range(peers):
        out[pl.ds(j * length, length), :] = packed


def third_body(slots, cols, arrived, gathered, total, tiles, spread, gather, out, residual_out, alpha_out):
    residual, weights = gathered[:, 0, :], gathered[:, 1, :]
    z = weights * residual
    group, size = residual.shape
    length = group * (size // LANES) + 1
    peers = arrived.shape[0] // length
    summed = arrived[pl.ds(0, length), :]
    for j in range(1, peers):
        summed += arrived[pl.ds(j * length, length), :]
    image = take(summed, group, size) + ridge_weight * z
    count = cols * (size // LANES)
    gamma = lane_sum(total[pl.ds(count, 1), :])
    curve = lane_sum(summed[length - 1 : length] + ridge_weight * total[pl.ds(count + 1, 1), :])
    alpha = gamma / curve
    alpha_out[...] = jnp.broadcast_to(alpha, alpha_out.shape)
    later = residual - alpha * image
    residual_out[...] = later
    z1 = weights * later
    put(out, count, fold(row_sum(later * z1)))
    put(out, count + 1, fold(row_sum(z1 * z1)))
    put(out, count + 2, fold(row_sum(z1 * z)))
    put(out, 0, block_product(spread, gather, z1, tiles.at[0, 0], slots))


def fourth_body(slots, by, p0, p1, p2, p3, total, gathered, residual, scaling, flipped, spread, gather, out, direction_out, scalars):
    summed = gather4((p0, p1, p2, p3))
    cols, size = scaling.shape
    count = cols * (size // LANES)
    gamma = lane_sum(total[pl.ds(count, 1), :])
    norm = lane_sum(total[pl.ds(count + 1, 1), :])
    later = lane_sum(summed[count : count + 1])
    beta = later / gamma
    square = lane_sum(summed[count + 1 : count + 2]) + beta * (2.0 * lane_sum(summed[count + 2 : count + 3]) + beta * norm)
    lifted = take(summed, cols, size) + beta * take(total[...], cols, size)
    weighted = scaling[...] * lifted
    inner = fold(row_sum(weighted * lifted))
    rows = block_product(spread, gather, weighted, flipped, slots)
    peers = out.shape[0]
    for h, piece in enumerate(pieces_of(rows)):
        out[:, h, :] = turned(piece, by)
    out[:, size // LANES, :] = jnp.broadcast_to(inner, (peers, LANES))
    weights = gathered[:, 1, :]
    direction_out[...] = weights * residual[...] + beta * (weights * gathered[:, 0, :])
    scalars[pl.ds(0, 1), :] = jnp.broadcast_to(later, (1, LANES))
    scalars[pl.ds(1, 1), :] = jnp.broadcast_to(square, (1, LANES))


def last_body(arrived, gathered, residual, direction, alpha, scalars, own, solution, residual_out):
    size = solution.shape[1]
    mask = own[:, :1]
    summed = jnp.sum(arrived[...], axis=0)
    image = take(summed, 1, size)
    curve = lane_sum(summed[size // LANES : size // LANES + 1]) + ridge_weight * scalars[1:2, :1]
    step = scalars[0:1, :1] / curve
    first = row_sum(mask * (gathered[:, 0, :] * gathered[:, 1, :]))
    second = row_sum(mask * direction[...])
    before = row_sum(mask * residual[...])
    solution[...] = alpha[:1, :1] * first + step * second
    residual_out[...] = before - step * (image + ridge_weight * second)


def turned(x, by):
    by %= x.shape[0]
    return jnp.concatenate([x[by:], x[:by]], axis=0) if by else x


def exchange(value, size, first):
    order = [(p + first) % size for p in range(size)]
    return lax.all_to_all(value, "col", 0, 0, tiled=True, axis_index_groups=[order])


def share(value, axis, size):
    moved = [value]
    for s in range(1, size):
        moved.append(lax.ppermute(value, axis, [(i, i ^ s) for i in range(size)]))
    return moved


def local(right_side, precond, scaling, blocks, block_count, block_rows, block_cols):
    peers = lax.axis_size("col")
    groups = lax.axis_size("row")
    slots, size = blocks.shape[2], blocks.shape[3]
    own_rows = right_side.shape[0]
    assert own_rows == 1 and groups == 4
    group = own_rows * peers
    cols = scaling.shape[0]
    pieces = size // LANES
    long = slots * size
    starts = [peers * f // 8 for f in FIRST]
    work = dict(flops=8 * long * size, moved=0)

    (own,) = call(
        lambda *refs: own_body(group, starts[0], *refs),
        "own",
        [((group, LANES), F32)],
        (),
        in_specs=[],
        flops=1 << 34,
    )
    sent, spread_rows, gather_cols = call(
        lambda *refs: start_body(group, slots, starts[0], *refs),
        "start",
        [((peers, 2, size), F32), ((3 * group, slots * LANES), BF16), ((cols, slots * 8), BF16)],
        (right_side, precond, block_count, block_rows, block_cols, own),
        in_specs=[vmem(), vmem(), pl.BlockSpec(memory_space=pltpu.SMEM), vmem(), vmem(), vmem()],
        flops=1 << 34,
        moved=100 << 20,
    )
    gathered = exchange(sent, peers, starts[0])
    (mine,) = call(
        lambda *refs: first_body(slots, cols, *refs),
        "first",
        [((cols * pieces + 2, 1, LANES), F32)],
        (gathered, blocks, spread_rows, gather_cols),
        **work,
    )
    plain = (slots - slots * SHARE // 16) // 2 * 2
    rest = slots - plain
    spread_cols, gather_rows, flipped = call(
        lambda *refs: flip_body(plain, group, cols, starts[0], *refs),
        "flip",
        [
            ((3 * cols, plain * LANES), BF16),
            ((group, plain * 8), BF16),
            ((plain, size, size), F32),
        ],
        (blocks, block_count, block_rows, block_cols),
        in_specs=[vmem(), pl.BlockSpec(memory_space=pltpu.SMEM), vmem(), vmem()],
        flops=FLIP,
    )
    length = group * pieces + 1
    total, sent = call(
        lambda *refs: second_body(plain, peers, *refs),
        "second",
        [((cols * pieces + 2, LANES), F32), ((peers * length, LANES), F32)],
        (*share(mine, "row", groups), scaling, flipped, spread_cols, gather_rows),
        **work,
    )
    arrived = exchange(sent.reshape(-1, 1, LANES), peers, starts[1])
    mine, residual, alpha = call(
        lambda *refs: third_body(plain, cols, *refs),
        "third",
        [((cols * pieces + 3, 1, LANES), F32), ((group, size), F32), ((1, LANES), F32)],
        (arrived.reshape(-1, LANES), gathered, total, blocks, spread_rows, gather_cols),
        **work,
    )
    sent, direction, scalars = call(
        lambda *refs: fourth_body(plain, starts[2] - starts[0], *refs),
        "fourth",
        [((peers, pieces + 1, LANES), F32), ((group, size), F32), ((2, LANES), F32)],
        (*share(mine, "row", groups), total, gathered, residual, scaling, flipped, spread_cols, gather_rows),
        **work,
    )
    arrived = exchange(sent, peers, starts[2])
    return pl.pallas_call(
        last_body,
        name="last",
        out_shape=[jax.ShapeDtypeStruct(right_side.shape, F32)] * 2,
        in_specs=[vmem()] * 7,
        out_specs=[vmem()] * 2,
        compiler_params=pltpu.CompilerParams(vmem_limit_bytes=VMEM_LIMIT),
    )(arrived, gathered, residual, direction, alpha, scalars, own)


def solution(mesh):
    placed = (
        P(("row", "col"), None),
        P(("row", "col"), None),
        P("col", None),
        P("col", "row", None, None, None),
        P("col", "row"),
        P("col", "row", None),
        P("col", "row", None),
    )
    return jax.shard_map(
        local,
        mesh=mesh,
        in_specs=placed,
        out_specs=(P(("row", "col"), None), P(("row", "col"), None)),
        check_vma=False,
    )
```
